256 devices in a mesh: section: 16 (over y, x), slab: 16 (over z, core).
Axes of the slice: x: 4, y: 4, z: 8, core: 2. Of those that a mesh axis runs over, the one named last changes fastest.
Arguments:
- features: bfloat16 [16, 16, 32, 2, 8, 256], P('section', None, 'slab'), may hold values from -40 to 40
- vae_weight: bfloat16 [3, 3, 3, 256, 256], replicated, may hold values from -0.078125 to 0.078125
- vae_gain: float32 [256], replicated, may hold values from 0.25 to 1.75
- vae_shift: float32 [256], replicated, may hold values from -3 to 3
- vae_bias: float32 [256], replicated, may hold values from -3 to 3
- latent_weight: bfloat16 [256, 16], replicated, may hold values from -0.375 to 0.375
- latent_bias: float32 [16], replicated, may hold values from -3 to 3
- slot_clips: int32 [16, 16], replicated, may hold values from 0 to 15, each once within a row
- row_offsets: int32 [16, 16], replicated, may hold values from 0 to 112
- in_weight: bfloat16 [3, 3, 16, 320], replicated, may hold values from -0.5 to 0.5
- in_bias: float32 [320], replicated, may hold values from -3 to 3
- pos_table: bfloat16 [128, 320], replicated, may hold values from -3 to 3
- unet_gain: float32 [16, 320], P('section'), may hold values from 0.25 to 1.75
- unet_shift: float32 [16, 320], P('section'), may hold values from -3 to 3
- unet_weight: bfloat16 [16, 3, 3, 320, 320], P('section'), may hold values from -0.109375 to 0.109375
- unet_bias: float32 [16, 320], P('section'), may hold values from -3 to 3
Outputs:
- layer_outputs: bfloat16 [16, 16, 16, 16, 2, 1280], P('section', None, 'slab')
The draws below stay inside these ranges and needn't reach their ends.
Inputs may be any that keep to these rules, and one draw needn't show every extreme that they name: Each row of slot_clips is a permutation of 0 to 15.
All inputs are finite; a program needn't handle non-finite values.
Results may differ from the reference program's by a relative error of at most 0.025.
Values may be sent and summed in bfloat16 or wider, within the bound.
A program may use at most 64 MiB of HBM per device.

```python
import jax
import jax.numpy as jnp
from jax import lax

CV = 256
CL = 16
CU = 320
GROUPS = 32
FRAMES = 2
FRAME_ROWS = 128
COLS = 8
MICRO = 16
LAYERS = 16
CLIPS = 16
ROWS = 32
LAT_ROWS = 16
LAT_COLS = 4


def draw_features(key, part):
    first_key, second_key = jax.random.split(key, 2)
    full_shape = (MICRO, CLIPS, ROWS, FRAMES, COLS, CV)
    row_frac = jnp.arange(ROWS, dtype=jnp.float32) / ROWS
    channel_draw = jax.random.uniform(second_key, (CV,), jnp.float32)
    basic_draw = jnp.clip(jax.random.normal(first_key, full_shape, jnp.float32), -6.0, 6.0)
    row_scale = 10.0 ** (row_frac - 0.5)
    channel_scale = 10.0 ** (0.5 * (channel_draw - 0.5))
    return (basic_draw * row_scale[:, None, None, None] * channel_scale).astype(jnp.bfloat16)


def set_ends(entries, rng, smallest, high):
    shape = entries.shape
    index_at = [jax.random.randint(jax.random.fold_in(rng, axis), (), 0, shape[axis]) for axis in range(len(shape))]
    entries = entries.at[tuple(index_at)].set(smallest)
    longest = shape.index(max(shape))
    index_at[longest] = (index_at[longest] + 1) % shape[longest]
    return entries.at[tuple(index_at)].set(high)


def block_levels(own_key, extent, cuts, low, largest):
    factor_of = 1.0
    for dim, shards_of in cuts:
        heights = jax.random.uniform(jax.random.fold_in(jax.random.fold_in(own_key, 6), dim), (shards_of,), jnp.float32, low / len(cuts), largest / len(cuts))
        factor_of = factor_of * jnp.repeat(jnp.exp(heights), extent[dim] // shards_of).reshape((-1,) + (1,) * (len(extent) - 1 - dim))
    return factor_of


def centred(key, extent, width, limit, cuts=(), kind=jnp.bfloat16):
    drawn = jax.random.normal(key, extent, jnp.float32) * width
    if len(cuts) > 0:
        drawn = block_levels(key, extent, cuts, -0.22, 0.18) * drawn
    return jnp.clip(drawn, min=-limit, max=limit).astype(kind)


def setup_inputs(seed: int = 0) -> dict:
    arg_keys = jax.random.split(jax.random.key(seed), 17)
    return {
        "features": draw_features(jax.random.fold_in(arg_keys[16], 71), 0),
        "vae_weight": centred(arg_keys[1], (3, 3, 3, CV, CV), (27 * CV) ** -0.5, 0.078125),
        "vae_gain": jnp.clip(1.0 + 0.15 * jax.random.normal(arg_keys[2], (CV,), jnp.float32), 0.25, 1.75),
        "vae_shift": centred(arg_keys[3], (CV,), 0.5, 3.0, (), jnp.float32),
        "vae_bias": centred(arg_keys[4], (CV,), 0.5, 3.0, (), jnp.float32),
        "latent_weight": centred(arg_keys[5], (CV, CL), CV ** -0.5, 0.375),
        "latent_bias": centred(arg_keys[6], (CL,), 0.5, 3.0, (), jnp.float32),
        "slot_clips": jax.vmap(lambda own: jax.random.permutation(own, CLIPS))(jax.random.split(arg_keys[7], MICRO)).reshape((MICRO, CLIPS)).astype(jnp.int32),
        "row_offsets": set_ends(jax.random.randint(arg_keys[8], (MICRO, CLIPS), 0, FRAME_ROWS - LAT_ROWS + 1), jax.random.fold_in(arg_keys[8], 1), 0, FRAME_ROWS - LAT_ROWS).astype(jnp.int32),
        "in_weight": centred(arg_keys[9], (3, 3, CL, CU), (9 * CL) ** -0.5, 0.5),
        "in_bias": centred(arg_keys[10], (CU,), 0.5, 3.0, (), jnp.float32),
        "pos_table": centred(arg_keys[11], (FRAME_ROWS, CU), 0.5, 3.0),
        "unet_gain": jnp.clip(1.0 + 0.15 * jax.random.normal(arg_keys[12], (LAYERS, CU), jnp.float32), 0.25, 1.75),
        "unet_shift": centred(arg_keys[13], (LAYERS, CU), 0.5, 3.0, ((0, 16),), jnp.float32),
        "unet_weight": centred(arg_keys[14], (LAYERS, 3, 3, CU, CU), (9 * CU) ** -0.5, 0.109375, ((0, 16),)),
        "unet_bias": centred(arg_keys[15], (LAYERS, CU), 0.5, 3.0, ((0, 16),), jnp.float32),
    }


norm_eps = 1e-06

def group_stats(values, groups):
    full_shape = values.shape
    grouped = values.reshape(full_shape[0], -1, groups, full_shape[-1] // groups)
    return (lax.optimization_barrier(jnp.sum(grouped, axis=(1, 3))), lax.optimization_barrier(jnp.sum(grouped * grouped, axis=(1, 3))))

def normalize(values, sums, squares, cell_count, gain, shift, groups):
    mean_value = sums / cell_count
    variance = squares / cell_count - mean_value * mean_value
    inverse = lax.rsqrt(variance + norm_eps)
    full_shape = values.shape
    grouped = values.reshape(full_shape[0], -1, groups, full_shape[-1] // groups)
    normed = (grouped - mean_value[:, None, :, None]) * inverse[:, None, :, None]
    return normed.reshape(full_shape) * gain + shift

def keep_stats(stats_pair):
    return stats_pair

def zero_rows(active):
    return jnp.pad(active, ((0, 0), (1, 1), (0, 0), (0, 0), (0, 0)))

def encode(features, rows_total, reduce_stats, extend_rows, encoder):
    vae_weight, vae_gain, vae_shift, vae_bias, latent_weight, latent_bias = encoder
    clip_count, rows_here, frame_count, col_count, channels = features.shape
    values = features.astype(jnp.float32)
    sums, squares = reduce_stats(group_stats(values, GROUPS))
    cell_count = rows_total * frame_count * col_count * (channels // GROUPS)
    normed = normalize(values, sums, squares, cell_count, vae_gain, vae_shift, GROUPS)
    active = jax.nn.silu(normed).astype(jnp.bfloat16)
    extended = extend_rows(active)
    first_frame = extended[:, :, :1]
    timed = jnp.concatenate([first_frame, first_frame, extended], axis=2)
    padded = jnp.pad(timed, ((0, 0), (0, 0), (0, 0), (1, 1), (0, 0)))
    mixed = jnp.zeros((clip_count * rows_here * frame_count * col_count, channels), jnp.float32)
    for time_tap in range(3):
        for row_tap in range(3):
            for col_tap in range(3):
                window = padded[:, row_tap:row_tap + rows_here, time_tap:time_tap + frame_count, col_tap:col_tap + col_count, :]
                mixed = mixed + jnp.dot(window.reshape(-1, channels), vae_weight[time_tap, row_tap, col_tap], preferred_element_type=jnp.float32)
    summed = values + mixed.reshape(values.shape) + vae_bias
    pooled = summed.reshape(clip_count, rows_here // 2, 2, frame_count, col_count // 2, 2, channels).mean(axis=(2, 5)).astype(jnp.bfloat16)
    latent = jnp.dot(pooled.reshape(-1, channels), latent_weight, preferred_element_type=jnp.float32) + latent_bias
    return latent.astype(jnp.bfloat16).reshape(clip_count, rows_here // 2, frame_count, col_count // 2, -1)

def spatial_conv(active, weight):
    clip_count, row_count, frame_count, col_count, channels = active.shape
    padded = jnp.pad(active, ((0, 0), (1, 1), (0, 0), (1, 1), (0, 0)))
    total = jnp.zeros((clip_count * row_count * frame_count * col_count, weight.shape[-1]), jnp.float32)
    for row_tap in range(3):
        for col_tap in range(3):
            window = padded[:, row_tap:row_tap + row_count, :, col_tap:col_tap + col_count, :]
            total = total + jnp.dot(window.reshape(-1, channels), weight[row_tap, col_tap], preferred_element_type=jnp.float32)
    return total.reshape(clip_count, row_count, frame_count, col_count, -1)

def embed(latent, offsets_now, in_weight, in_bias, pos_table):
    projected = spatial_conv(latent, in_weight) + in_bias
    row_count = latent.shape[1]
    table_rows = pos_table.shape[0]
    wanted = offsets_now[:, None] + jnp.arange(row_count, dtype=jnp.int32)[None, :]
    one_hot = (wanted[:, :, None] == jnp.arange(table_rows, dtype=jnp.int32)[None, None, :]).astype(jnp.bfloat16)
    placed = jnp.dot(one_hot.reshape(-1, table_rows), pos_table, preferred_element_type=jnp.float32)
    placed = placed.reshape(latent.shape[0], row_count, 1, 1, -1)
    return (projected + placed).astype(jnp.bfloat16)

def unet_layer(state, gain, shift, weight, bias):
    values = state.astype(jnp.float32)
    sums, squares = group_stats(values, GROUPS)
    cell_count = values.shape[1] * values.shape[2] * values.shape[3] * (values.shape[4] // GROUPS)
    normed = normalize(values, sums, squares, cell_count, gain, shift, GROUPS)
    active = jax.nn.silu(normed).astype(jnp.bfloat16)
    return (values + spatial_conv(active, weight) + bias).astype(jnp.bfloat16)

def reference(features, vae_weight, vae_gain, vae_shift, vae_bias, latent_weight, latent_bias, slot_clips, row_offsets, in_weight, in_bias, pos_table, unet_gain, unet_shift, unet_weight, unet_bias):
    encoder = (vae_weight, vae_gain, vae_shift, vae_bias, latent_weight, latent_bias)

    def per_micro(micro_index):
        micro_batch = lax.dynamic_index_in_dim(features, micro_index, 0, keepdims=False)
        latent = encode(micro_batch, micro_batch.shape[1], keep_stats, zero_rows, encoder)
        order = lax.dynamic_index_in_dim(slot_clips, micro_index, 0, keepdims=False)
        ordered = jnp.take(latent, order, axis=0)
        offsets_row = lax.dynamic_index_in_dim(row_offsets, micro_index, 0, keepdims=False)
        state = embed(ordered, jnp.take(offsets_row, order), in_weight, in_bias, pos_table)
        outputs = []
        for layer_index in range(LAYERS):
            state = unet_layer(state, unet_gain[layer_index], unet_shift[layer_index], unet_weight[layer_index], unet_bias[layer_index])
            outputs.append(state)
        return jnp.stack(outputs)
    stacked = lax.map(per_micro, jnp.arange(MICRO, dtype=jnp.int32))
    stacked = jnp.transpose(stacked, (1, 0, 2, 3, 4, 5, 6))
    return stacked.reshape(LAYERS, MICRO, CLIPS, LAT_ROWS, FRAMES, LAT_COLS * CU)
```

```python
import jax
import jax.numpy as jnp
from jax import lax
from jax.experimental import pallas as pl
from jax.experimental.pallas import tpu as pltpu
from jax.sharding import PartitionSpec as P

BF = jnp.bfloat16
F32 = jnp.float32
MESH = pl.DeviceIdType.MESH
EPS = 1e-6
SIDE = 4
PIECE = 240


def group_matrix(used, width, group):
    a = lax.broadcasted_iota(jnp.int32, (width, width), 0)
    b = lax.broadcasted_iota(jnp.int32, (width, width), 1)
    same = (b - b % group) == (a - a % group)
    hit = jnp.logical_and(same, jnp.logical_and(a < used, b < used))
    return jnp.where(hit, 1.0, 0.0).astype(BF)


def group_stats(values, members, count):
    first = jnp.sum(jnp.sum(values, axis=0), axis=0, keepdims=True)
    second = jnp.sum(jnp.sum(values * values, axis=0), axis=0, keepdims=True)
    parts = []
    for total in (first, second):
        high = total.astype(BF).astype(F32)
        rest = total - high
        mid = rest.astype(BF).astype(F32)
        parts += [high, mid, rest - mid]
    width = values.shape[-1]
    row = lax.broadcasted_iota(jnp.int32, (8, width), 0)
    left = jnp.zeros((8, width), F32)
    for index, part in enumerate(parts):
        left = jnp.where(row == index, part, left)
    sums = jnp.dot(left.astype(BF), members, preferred_element_type=F32)
    mean = (sums[0:1] + sums[1:2] + sums[2:3]) * (1.0 / count)
    meansq = (sums[3:4] + sums[4:5] + sums[5:6]) * (1.0 / count)
    return mean, lax.rsqrt(meansq - mean * mean + EPS)


def silu(v):
    half = 0.5 * v
    return half + half * jnp.tanh(half)


def up_down(values):
    zero = jnp.zeros_like(values[:1])
    return (
        jnp.concatenate([zero, values[:-1]], axis=0),
        jnp.concatenate([values[1:], zero], axis=0),
    )


def beside(values, step, cols):
    col = lax.broadcasted_iota(jnp.int32, values.shape, 1) % cols
    edge = 0 if step == 1 else cols - 1
    return jnp.where(col == edge, 0.0, pltpu.roll(values, step % 8, 1))


def block(y, gain, shift, bias, weight, members):
    mean, inverse = group_stats(y, members, 1280)
    act = silu((y - mean) * (inverse * gain) + shift)
    above, below = (a.reshape(128, 384) for a in up_down(act))
    here = act.reshape(128, 384)
    low = lax.broadcasted_iota(jnp.int32, (128, 128), 1) < 64
    tail = jnp.where(low, above[:, 256:], pltpu.roll(here[:, 256:], 64, 1))
    pieces = (above[:, :256], here[:, :256], below[:, :256], tail, below[:, 256:])
    left = jnp.concatenate([a.astype(BF) for a in pieces], axis=1)

    def product(n):
        return jnp.dot(left, weight[:, n * 256 : (n + 1) * 256], preferred_element_type=F32)

    def joined(main, end):
        return jnp.concatenate([main, end], axis=1).reshape(16, 8, 384)

    tails = product(3)
    ends = tails[:, :128]
    before = joined(product(0), jnp.where(low, pltpu.roll(ends, 64, 1), 0.0))
    middle = joined(product(1), jnp.where(low, ends, 0.0))
    after = joined(product(2), tails[:, 128:])
    out = y + middle + beside(before, 1, 4) + beside(after, -1, 4) + bias
    return out.astype(BF)


def pack_weight(raw, packed):
    packed[960:1024, :] = jnp.zeros((64, 1024), BF)
    for tap in range(3):
        for first, count, start in ((0, 256, tap * 256), (256, 64, 768 + 64 * tap)):
            rows = slice(start, start + count)
            ends = []
            for e in range(3):
                source = raw.at[tap * 3 + e]
                packed[rows, e * 256 : (e + 1) * 256] = source[first : first + count, :256]
                ends.append(source[first : first + count, 256:])
            packed[rows, 768:896] = jnp.concatenate([ends[1], ends[0]], axis=1)
            packed[rows, 896:1024] = jnp.concatenate([ends[2], jnp.zeros_like(ends[2])], axis=1)


def encode(clip, gain, shift, bias, weight, latent_weight, latent_bias):
    members = group_matrix(256, 256, 8)
    values = clip.astype(F32).reshape(64, 8, 256)
    mean, inverse = group_stats(values, members, 4096)
    act = silu((values - mean) * (inverse * gain) + shift).reshape(32, 2, 8, 256)
    lefts = []
    for frame in range(2):
        here = act[:, frame]
        above, below = up_down(here)
        lefts.append(
            jnp.concatenate([a.reshape(256, 256).astype(BF) for a in (above, here, below)], axis=1)
        )
    both = jnp.concatenate(lefts, axis=0)
    sums = [jnp.zeros((32, 8, 256), F32)] * 2
    for e in range(3):
        shared = jnp.dot(
            lefts[0], weight[e, 0:768, :], preferred_element_type=F32
        ) + jnp.dot(lefts[0], weight[e, 768:1536, :], preferred_element_type=F32)
        own = jnp.dot(both, weight[e, 1536:2304, :], preferred_element_type=F32)
        for frame in range(2):
            part = (shared + own[frame * 256 : (frame + 1) * 256]).reshape(32, 8, 256)
            sums[frame] = sums[frame] + (part if e == 1 else beside(part, 1 - e, 8))
    values = values.reshape(32, 2, 8, 256)
    paired = []
    for frame in range(2):
        summed = (values[:, frame] + sums[frame] + bias).reshape(16, 2, 8, 256)
        paired.append(summed[:, 0] + summed[:, 1])
    stacked = jnp.stack(paired, axis=1).reshape(256, 256)
    terms = []
    for _ in range(3):
        high = stacked.astype(BF)
        terms.append(high)
        stacked = stacked - high.astype(F32)
    row = lax.broadcasted_iota(jnp.int32, (128, 256), 0)
    col = lax.broadcasted_iota(jnp.int32, (128, 256), 1)
    pick = jnp.where(col - col % 2 == 2 * row, 1.0, 0.0).astype(BF)
    total = jnp.zeros((128, 256), F32)
    for high in terms:
        total = total + jnp.dot(pick, high, preferred_element_type=F32)
    pooled = (0.25 * total).astype(BF)
    latent = jnp.dot(pooled, latent_weight, preferred_element_type=F32) + latent_bias
    return latent.astype(BF).astype(F32)


def embed(latent, offset, weight, bias, table):
    grid = latent.reshape(16, 8, 16)
    columns = (beside(grid, 1, 4), grid, beside(grid, -1, 4))
    total = jnp.zeros((128, 320), F32)
    for e in range(3):
        above, below = up_down(columns[e])
        for b, rows in enumerate((above, columns[e], below)):
            total = total + jnp.dot(
                rows.reshape(128, 16).astype(BF), weight[b * 3 + e], preferred_element_type=F32
            )
    row = lax.broadcasted_iota(jnp.int32, (16, 8, 128), 0)
    entry = lax.broadcasted_iota(jnp.int32, (16, 8, 128), 2)
    one_hot = jnp.where(entry == row + offset, 1.0, 0.0).reshape(128, 128).astype(BF)
    placed = jnp.dot(one_hot, table, preferred_element_type=F32)
    return (total + bias + placed).astype(BF)


def kernel(
    slots,
    offsets,
    features,
    vae_weight,
    vae_gain,
    vae_shift,
    vae_bias,
    latent_weight,
    latent_bias,
    in_weight,
    in_bias,
    table,
    gain,
    shift,
    bias,
    unet_weight,
    out,
    staged,
    clip,
    encoder,
    raw,
    packed,
    norms,
    first_state,
    arriving,
    leaving,
    results,
    state,
    spread,
    members,
    load_sem,
    clip_send,
    clip_recv,
    norm_send,
    norm_recv,
    ring_send,
    ring_recv,
    twin_send,
    twin_recv,
    first_send,
    state_send,
    state_recv,
    out_send,
    out_recv,
    keep_sem,
):
    section = lax.axis_index("section")
    slab = lax.axis_index("slab")
    x, y = section % SIDE, section // SIDE
    core = slab % 2
    twin = slab + 1 - 2 * core

    def at_x(step):
        return {"section": y * SIDE + (x + step + SIDE) % SIDE}

    weight_load = pltpu.make_async_copy(unet_weight, raw, load_sem.at[27])
    weight_load.start()

    def encoder_load(tap):
        a, b, e = tap // 9, (tap // 3) % 3, tap % 3
        return pltpu.make_async_copy(
            vae_weight.at[tap],
            encoder.at[e, pl.ds(a * 768 + b * 256, 256), :],
            load_sem.at[tap],
        )

    @pl.loop(0, 27)
    def _(tap):
        encoder_load(tap).start()

    barrier = pltpu.get_barrier_semaphore()

    @pl.loop(1, SIDE)
    def _(step):
        pl.semaphore_signal(barrier, 1, device_id=at_x(step), device_id_type=MESH)
        pl.semaphore_signal(
            barrier,
            1,
            device_id={"section": ((y + step) % SIDE) * SIDE + x},
            device_id_type=MESH,
        )

    @pl.loop(1, 16)
    def _(step):
        pl.semaphore_signal(
            barrier, 1, device_id={"slab": (slab + step) % 16}, device_id_type=MESH
        )

    @pl.loop(0, 16)
    def _(slot):
        staged[slot] = features[slots[section, slot]]

    members[...] = group_matrix(320, 384, 10)
    norms[x] = jnp.zeros((8, 384), F32)
    norms[x, 0:1, 0:320] = gain[...]
    norms[x, 1:2, 0:320] = shift[...]
    norms[x, 2:3, 0:320] = bias[...]
    first_state[...] = jnp.zeros((128, 384), BF)
    weight_load.wait()
    pack_weight(raw, packed.at[x])
    for other in range(1, SIDE):
        packed[(x + other) % SIDE, 960:1024, :] = jnp.zeros((64, 1024), BF)
    pl.semaphore_wait(barrier, 21)

    def clip_copy(step):
        return pltpu.make_async_remote_copy(
            src_ref=staged.at[(slab + step) % 16],
            dst_ref=clip.at[slab],
            send_sem=clip_send.at[step],
            recv_sem=clip_recv.at[step],
            device_id={"slab": (slab + step) % 16},
            device_id_type=MESH,
        )

    def clip_arrival(step):
        return pltpu.make_async_remote_copy(
            src_ref=staged.at[slab],
            dst_ref=clip.at[(slab + 16 - step) % 16],
            send_sem=clip_send.at[step],
            recv_sem=clip_recv.at[step],
            device_id={"slab": (slab + step) % 16},
            device_id_type=MESH,
        )

    @pl.loop(1, 16)
    def _(step):
        clip_copy(step).start()

    def piece(way, owner, which):
        rows = pl.ds(pl.multiple_of((way * 2 + which) * PIECE, 16), PIECE)
        return packed.at[owner, rows, :]

    def ring_copy(way, step):
        sign = 1 - 2 * way
        mine = piece(way, (x - sign * step + SIDE) % SIDE, core)
        return pltpu.make_async_remote_copy(
            src_ref=mine,
            dst_ref=mine,
            send_sem=ring_send.at[way, step],
            recv_sem=ring_recv.at[way, step],
            device_id=at_x(sign),
            device_id_type=MESH,
        )

    def ring_arrival(way, step):
        sign = 1 - 2 * way
        theirs = piece(way, (x - sign * (step + 1) + SIDE) % SIDE, core)
        return pltpu.make_async_remote_copy(
            src_ref=theirs,
            dst_ref=theirs,
            send_sem=ring_send.at[way, step],
            recv_sem=ring_recv.at[way, step],
            device_id=at_x(sign),
            device_id_type=MESH,
        )

    def twin_copy(way, step, which):
        sign = 1 - 2 * way
        block_at = piece(way, (x - sign * (step + 1) + SIDE) % SIDE, which)
        return pltpu.make_async_remote_copy(
            src_ref=block_at,
            dst_ref=block_at,
            send_sem=twin_send.at[way, step],
            recv_sem=twin_recv.at[way, step],
            device_id={"slab": twin},
            device_id_type=MESH,
        )

    def norm_copy(step, owner):
        return pltpu.make_async_remote_copy(
            src_ref=norms.at[owner],
            dst_ref=norms.at[owner],
            send_sem=norm_send.at[step],
            recv_sem=norm_recv.at[step],
            device_id=at_x(step),
            device_id_type=MESH,
        )

    for way in range(2):
        ring_copy(way, 0).start()

    @pl.loop(1, SIDE)
    def _(step):
        norm_copy(step, x).start()

    clip[slab] = staged[slab]

    @pl.loop(0, 27)
    def _(tap):
        encoder_load(tap).wait()

    @pl.loop(1, 16)
    def _(step):
        clip_arrival(step).wait_recv()

    latent = encode(
        clip[...].reshape(512, 256),
        vae_gain[...],
        vae_shift[...],
        vae_bias[...],
        encoder,
        latent_weight[...],
        latent_bias[...],
    )
    offset = offsets[section, slots[section, slab]]
    first_state[:, 0:320] = embed(latent, offset, in_weight, in_bias[...], table[...])

    def first_copy():
        return pltpu.make_async_remote_copy(
            src_ref=first_state,
            dst_ref=arriving.at[y],
            send_sem=first_send,
            recv_sem=state_recv.at[y],
            device_id={"section": x},
            device_id_type=MESH,
        )

    @pl.when(y == 0)
    def _():
        arriving[0] = first_state[...]

    @pl.when(y > 0)
    def _():
        first_copy().start()

    for step in range(3):
        for way in range(2):
            ring_arrival(way, step).wait_recv()
            if step < 2:
                ring_copy(way, step + 1).start()
            twin_copy(way, step, core).start()

    @pl.loop(1, SIDE)
    def _(step):
        norm_copy(step, (x + SIDE - step) % SIDE).wait_recv()

    for step in range(3):
        for way in range(2):
            twin_copy(way, step, 1 - core).wait_recv()

    def state_copy(turn):
        return pltpu.make_async_remote_copy(
            src_ref=leaving.at[turn],
            dst_ref=arriving.at[turn],
            send_sem=state_send.at[turn],
            recv_sem=state_recv.at[turn],
            device_id={"section": (section + SIDE) % 16},
            device_id_type=MESH,
        )

    def out_copy(index):
        turn, layer = index // SIDE, index % SIDE
        return pltpu.make_async_remote_copy(
            src_ref=results.at[index],
            dst_ref=out.at[turn * SIDE + x],
            send_sem=out_send.at[index],
            recv_sem=out_recv.at[turn * SIDE + x],
            device_id={"section": y * SIDE + layer},
            device_id_type=MESH,
        )

    def out_arrival(micro):
        return pltpu.make_async_remote_copy(
            src_ref=results.at[micro],
            dst_ref=out.at[micro],
            send_sem=out_send.at[micro],
            recv_sem=out_recv.at[micro],
            device_id={"section": y * SIDE + micro % SIDE},
            device_id_type=MESH,
        )

    def keep_copy(turn):
        index = turn * SIDE + x
        return pltpu.make_async_copy(results.at[index], out.at[index], keep_sem.at[turn])

    @pl.loop(0, 16)
    def _(index):
        turn, layer = index // SIDE, index % SIDE

        @pl.when(jnp.logical_and(layer == 0, turn + y > 0))
        def _():
            state_copy(turn).wait_recv()

        @pl.when(layer == 0)
        def _():
            state[...] = arriving[turn].astype(F32).reshape(16, 8, 384)

        result = block(
            state[...],
            norms[layer, 0:1, :],
            norms[layer, 1:2, :],
            norms[layer, 2:3, :],
            packed.at[layer],
            members[...],
        )

        @pl.when(jnp.logical_and(layer == SIDE - 1, y < SIDE - 1))
        def _():
            leaving[turn] = result.reshape(128, 384)
            state_copy(turn).start()

        result = result.astype(F32)
        state[...] = result
        for n in range(3):
            spread[n] = result[:, :, n * 128 : (n + 1) * 128].reshape(128, 128)
        cells = []
        for col in range(4):
            every = pl.ds(col, 32, stride=4)
            cells += [spread[0, every, :], spread[1, every, :], spread[2, every, :][:, :64]]
        results[index] = jnp.concatenate(cells, axis=1).astype(BF)

        @pl.when(layer == x)
        def _():
            keep_copy(turn).start()

        @pl.when(layer != x)
        def _():
            out_copy(index).start()

    @pl.loop(0, 16)
    def _(index):
        @pl.when(index % SIDE != x)
        def _():
            out_copy(index).wait_send()
            out_arrival(index).wait_recv()

    @pl.loop(0, SIDE)
    def _(turn):
        keep_copy(turn).wait()

        @pl.when(y < SIDE - 1)
        def _():
            state_copy(turn).wait_send()

    @pl.when(y > 0)
    def _():
        first_copy().wait_send()

    @pl.loop(1, 16)
    def _(step):
        clip_copy(step).wait_send()

    @pl.loop(1, SIDE)
    def _(step):
        norm_copy(step, x).wait_send()

    for step in range(3):
        for way in range(2):
            ring_copy(way, step).wait_send()
            twin_copy(way, step, core).wait_send()


def per_device(
    features,
    vae_weight,
    vae_gain,
    vae_shift,
    vae_bias,
    latent_weight,
    latent_bias,
    slot_clips,
    row_offsets,
    in_weight,
    in_bias,
    pos_table,
    unet_gain,
    unet_shift,
    unet_weight,
    unet_bias,
):
    vmem = pl.BlockSpec(memory_space=pltpu.VMEM)
    smem = pl.BlockSpec(memory_space=pltpu.SMEM)
    anywhere = pl.BlockSpec(memory_space=pl.ANY)
    dma = pltpu.SemaphoreType.DMA
    result = pl.pallas_call(
        kernel,
        out_shape=jax.ShapeDtypeStruct((16, 32, 1280), BF),
        in_specs=[smem, smem, vmem, anywhere] + [vmem] * 11 + [anywhere],
        out_specs=anywhere,
        scratch_shapes=[
            pltpu.VMEM((16, 32, 256), BF),
            pltpu.VMEM((16, 32, 256), BF),
            pltpu.VMEM((3, 2304, 256), BF),
            pltpu.VMEM((9, 320, 320), BF),
            pltpu.VMEM((SIDE, 1024, 1024), BF),
            pltpu.VMEM((SIDE, 8, 384), F32),
            pltpu.VMEM((128, 384), BF),
            pltpu.VMEM((SIDE, 128, 384), BF),
            pltpu.VMEM((SIDE, 128, 384), BF),
            pltpu.VMEM((16, 32, 1280), BF),
            pltpu.VMEM((16, 8, 384), F32),
            pltpu.VMEM((3, 128, 128), F32),
            pltpu.VMEM((384, 384), BF),
            dma((28,)),
            dma((16,)),
            dma((16,)),
            dma((SIDE,)),
            dma((SIDE,)),
            dma((2, 3)),
            dma((2, 3)),
            dma((2, 3)),
            dma((2, 3)),
            dma,
            dma((SIDE,)),
            dma((SIDE,)),
            dma((16,)),
            dma((16,)),
            dma((SIDE,)),
        ],
        compiler_params=pltpu.CompilerParams(
            collective_id=0, has_side_effects=True, vmem_limit_bytes=48 * 1024 * 1024
        ),
    )(
        slot_clips,
        row_offsets,
        features.reshape(16, 32, 256),
        vae_weight.reshape(27, 256, 256),
        vae_gain.reshape(1, 256),
        vae_shift.reshape(1, 256),
        vae_bias.reshape(1, 256),
        latent_weight,
        latent_bias.reshape(1, 16),
        in_weight.reshape(9, 16, 320),
        in_bias.reshape(1, 320),
        pos_table,
        unet_gain,
        unet_shift,
        unet_bias,
        unet_weight.reshape(9, 320, 320),
    )
    return result.reshape(1, 16, 1, 16, 2, 1280)


def solution(mesh):
    return jax.shard_map(
        per_device,
        mesh=mesh,
        in_specs=(
            P("section", None, "slab", None, None, None),
            P(),
            P(),
            P(),
            P(),
            P(),
            P(),
            P(),
            P(),
            P(),
            P(),
            P(),
            P("section", None),
            P("section", None),
            P("section", None, None, None, None),
            P("section", None),
        ),
        out_specs=P("section", None, "slab", None, None, None),
        check_vma=False,
    )
```

```python
import jax
import jax.numpy as jnp
from jax import lax
from jax.experimental import pallas as pl
from jax.experimental.pallas import tpu as pltpu
from jax.sharding import PartitionSpec as P

BF = jnp.bfloat16
F32 = jnp.float32
MESH = pl.DeviceIdType.MESH
EPS = 1e-6
SIDE = 4
QUARTER = 240
CHUNKS = ((0, 64), (64, 64), (128, 64), (192, 48))


def group_matrix(used, width, group):
    a = lax.broadcasted_iota(jnp.int32, (width, width), 0)
    b = lax.broadcasted_iota(jnp.int32, (width, width), 1)
    same = (b - b % group) == (a - a % group)
    hit = jnp.logical_and(same, jnp.logical_and(a < used, b < used))
    return jnp.where(hit, 1.0, 0.0).astype(BF)


def group_stats(values, members, count):
    first = jnp.sum(jnp.sum(values, axis=0), axis=0, keepdims=True)
    second = jnp.sum(jnp.sum(values * values, axis=0), axis=0, keepdims=True)
    parts = []
    for total in (first, second):
        high = total.astype(BF).astype(F32)
        rest = total - high
        mid = rest.astype(BF).astype(F32)
        parts += [high, mid, rest - mid]
    width = values.shape[-1]
    row = lax.broadcasted_iota(jnp.int32, (8, width), 0)
    left = jnp.zeros((8, width), F32)
    for index, part in enumerate(parts):
        left = jnp.where(row == index, part, left)
    sums = jnp.dot(left.astype(BF), members, preferred_element_type=F32)
    mean = (sums[0:1] + sums[1:2] + sums[2:3]) * (1.0 / count)
    meansq = (sums[3:4] + sums[4:5] + sums[5:6]) * (1.0 / count)
    return mean, lax.rsqrt(meansq - mean * mean + EPS)


def silu(v):
    half = 0.5 * v
    return half + half * jnp.tanh(half)


def across(left, right):
    return lax.dot_general(left, right, (((1,), (1,)), ((), ())), preferred_element_type=F32)


def up_down(values):
    zero = jnp.zeros_like(values[:1])
    return (
        jnp.concatenate([zero, values[:-1]], axis=0),
        jnp.concatenate([values[1:], zero], axis=0),
    )


def beside(values, step, cols):
    col = lax.broadcasted_iota(jnp.int32, values.shape, 1) % cols
    edge = 0 if step == 1 else cols - 1
    return jnp.where(col == edge, 0.0, pltpu.roll(values, step % 8, 1))


def block(y, gain, shift, bias, weight, members):
    mean, inverse = group_stats(y, members, 1280)
    act = silu((y - mean) * (inverse * gain) + shift)
    above, below = (a.reshape(128, 384) for a in up_down(act))
    here = act.reshape(128, 384)
    low = lax.broadcasted_iota(jnp.int32, (128, 128), 1) < 64
    tail = jnp.where(low, above[:, 256:], pltpu.roll(here[:, 256:], 64, 1))
    pieces = (above[:, :256], here[:, :256], below[:, :256], tail, below[:, 256:])
    left = jnp.concatenate([a.astype(BF) for a in pieces], axis=1)

    def product(n):
        return jnp.dot(left, weight[:, n * 256 : (n + 1) * 256], preferred_element_type=F32)

    def joined(main, end):
        return jnp.concatenate([main, end], axis=1).reshape(16, 8, 384)

    tails = product(3)
    ends = tails[:, :128]
    before = joined(product(0), jnp.where(low, pltpu.roll(ends, 64, 1), 0.0))
    middle = joined(product(1), jnp.where(low, ends, 0.0))
    after = joined(product(2), tails[:, 128:])
    out = y + middle + beside(before, 1, 4) + beside(after, -1, 4) + bias
    return out.astype(BF)


def pack_weight(raw, packed):
    packed[960:1024, :] = jnp.zeros((64, 1024), BF)
    for tap in range(3):
        for first, count, start in ((0, 256, tap * 256), (256, 64, 768 + 64 * tap)):
            rows = slice(start, start + count)
            ends = []
            for e in range(3):
                source = raw.at[tap * 3 + e]
                packed[rows, e * 256 : (e + 1) * 256] = source[first : first + count, :256]
                ends.append(source[first : first + count, 256:])
            packed[rows, 768:896] = jnp.concatenate([ends[1], ends[0]], axis=1)
            packed[rows, 896:1024] = jnp.concatenate([ends[2], jnp.zeros_like(ends[2])], axis=1)


def encode(clip, gain, shift, bias, weight, latent_weight, latent_bias):
    members = group_matrix(256, 256, 8)
    values = clip.astype(F32).reshape(64, 8, 256)
    mean, inverse = group_stats(values, members, 4096)
    act = silu((values - mean) * (inverse * gain) + shift).reshape(32, 2, 8, 256)
    lefts = []
    for frame in range(2):
        here = act[:, frame]
        above, below = up_down(here)
        lefts.append(
            jnp.concatenate([a.reshape(256, 256).astype(BF) for a in (above, here, below)], axis=1)
        )
    both = jnp.concatenate(lefts, axis=0)
    sums = [jnp.zeros((32, 8, 256), F32)] * 2
    for e in range(3):
        shared = jnp.dot(
            lefts[0], weight[e, 0:768, :], preferred_element_type=F32
        ) + jnp.dot(lefts[0], weight[e, 768:1536, :], preferred_element_type=F32)
        own = jnp.dot(both, weight[e, 1536:2304, :], preferred_element_type=F32)
        for frame in range(2):
            part = (shared + own[frame * 256 : (frame + 1) * 256]).reshape(32, 8, 256)
            sums[frame] = sums[frame] + (part if e == 1 else beside(part, 1 - e, 8))
    values = values.reshape(32, 2, 8, 256)
    paired = []
    for frame in range(2):
        summed = (values[:, frame] + sums[frame] + bias).reshape(16, 2, 8, 256)
        paired.append(summed[:, 0] + summed[:, 1])
    stacked = jnp.stack(paired, axis=1).reshape(256, 256)
    terms = []
    for _ in range(3):
        high = stacked.astype(BF)
        terms.append(high)
        stacked = stacked - high.astype(F32)
    row = lax.broadcasted_iota(jnp.int32, (128, 256), 0)
    col = lax.broadcasted_iota(jnp.int32, (128, 256), 1)
    pick = jnp.where(col - col % 2 == 2 * row, 1.0, 0.0).astype(BF)
    total = jnp.zeros((128, 256), F32)
    for high in terms:
        total = total + jnp.dot(pick, high, preferred_element_type=F32)
    pooled = (0.25 * total).astype(BF)
    latent = across(pooled, latent_weight) + latent_bias
    return latent.astype(BF).astype(F32)


def embed(latent, offset, weight, bias, table):
    grid = latent.reshape(16, 8, 16)
    columns = (beside(grid, 1, 4), grid, beside(grid, -1, 4))
    total = jnp.zeros((128, 320), F32)
    for e in range(3):
        above, below = up_down(columns[e])
        for b, rows in enumerate((above, columns[e], below)):
            total = total + jnp.dot(
                rows.reshape(128, 16).astype(BF), weight[b * 3 + e], preferred_element_type=F32
            )
    row = lax.broadcasted_iota(jnp.int32, (16, 8, 128), 0)
    entry = lax.broadcasted_iota(jnp.int32, (16, 8, 128), 2)
    one_hot = jnp.where(entry == row + offset, 1.0, 0.0).reshape(128, 128).astype(BF)
    placed = across(one_hot, table)
    return (total + bias + placed).astype(BF)


def kernel(
    slots_in,
    offsets_in,
    features_in,
    vae_weight,
    vae_gain_in,
    vae_shift_in,
    vae_bias_in,
    latent_weight_in,
    latent_bias_in,
    in_weight_in,
    in_bias_in,
    table_in,
    gain_in,
    shift_in,
    bias_in,
    unet_weight,
    out,
    slots,
    offsets,
    features,
    vae_gain,
    vae_shift,
    vae_bias,
    latent_weight,
    latent_bias,
    in_weight,
    in_bias,
    table,
    gain,
    shift,
    bias,
    staged,
    clip,
    encoder,
    raw,
    packed,
    norms,
    first_state,
    arriving,
    leaving,
    results,
    state,
    spread,
    members,
    load_sem,
    small_sem,
    clip_send,
    clip_recv,
    norm_send,
    norm_recv,
    ring_send,
    ring_recv,
    pair_send,
    pair_recv,
    twin_send,
    twin_recv,
    first_send,
    state_send,
    state_recv,
    out_send,
    out_recv,
    keep_sem,
):
    section = lax.axis_index("section")
    slab = lax.axis_index("slab")
    x, y = section % SIDE, section // SIDE
    core = slab % 2
    parity = (slab // 2) % 2
    twin = slab + 1 - 2 * core

    def at_x(step):
        return {"section": y * SIDE + (x + step + SIDE) % SIDE}

    def remote(source, target, send, recv, device):
        return pltpu.make_async_remote_copy(
            src_ref=source,
            dst_ref=target,
            send_sem=send,
            recv_sem=recv,
            device_id=device,
            device_id_type=MESH,
        )

    weight_load = pltpu.make_async_copy(unet_weight, raw, load_sem.at[27])
    small = [
        pltpu.make_async_copy(source, target, small_sem.at[index])
        for index, (source, target) in enumerate(
            (
                (slots_in, slots),
                (offsets_in, offsets),
                (features_in, features),
                (gain_in, gain),
                (shift_in, shift),
                (bias_in, bias),
                (vae_gain_in, vae_gain),
                (vae_shift_in, vae_shift),
                (vae_bias_in, vae_bias),
                (latent_weight_in, latent_weight),
                (latent_bias_in, latent_bias),
                (in_weight_in, in_weight),
                (in_bias_in, in_bias),
                (table_in, table),
            )
        )
    ]

    def encoder_load(tap):
        a, b, e = tap // 9, (tap // 3) % 3, tap % 3
        return pltpu.make_async_copy(
            vae_weight.at[tap],
            encoder.at[e, pl.ds(a * 768 + b * 256, 256), :],
            load_sem.at[tap],
        )

    barrier = pltpu.get_barrier_semaphore()

    def greet(device):
        pl.semaphore_signal(barrier, 1, device_id=device, device_id_type=MESH)

    @pl.loop(1, 16)
    def _(step):
        greet({"slab": (slab + step) % 16})

    @pl.loop(1, SIDE)
    def _(step):
        greet(at_x(step))
        greet({"section": ((y + step) % SIDE) * SIDE + x})

    weight_load.start()
    for copy in small:
        copy.start()

    @pl.loop(0, 27)
    def _(tap):
        encoder_load(tap).start()

    members[...] = group_matrix(320, 384, 10)
    first_state[...] = jnp.zeros((128, 384), BF)
    for layer in range(SIDE):
        packed[layer, 960:1024, :] = jnp.zeros((64, 1024), BF)
    norms[x] = jnp.zeros((8, 384), F32)
    weight_load.wait()
    pack_weight(raw, packed.at[x])
    for copy in small:
        copy.wait()
    norms[x, 0:1, 0:320] = gain[...]
    norms[x, 1:2, 0:320] = shift[...]
    norms[x, 2:3, 0:320] = bias[...]

    @pl.loop(0, 16)
    def _(slot):
        staged[slot] = features[slots[section, slot]]

    pl.semaphore_wait(barrier, 21)

    def chunk(owner, side, which, index):
        first, count = CHUNKS[index]
        start = (side * 2 + which) * QUARTER + first
        return packed.at[owner, pl.ds(pl.multiple_of(start, 16), count), :]

    def ring_copy(distance, index, from_left):
        step = 1 if from_left else -1
        owner = (x + step - distance + 2 * SIDE) % SIDE
        mine = chunk(owner, parity, core, index)
        at = (distance - 1) * 4 + index
        return remote(mine, mine, ring_send.at[at], ring_recv.at[at], at_x(step))

    def moved(distance, index, side, which, sems, device):
        owner = (x - distance + SIDE) % SIDE
        mine = chunk(owner, side, which, index)
        at = (distance - 1) * 4 + index
        return remote(mine, mine, sems[0].at[at], sems[1].at[at], device)

    ring = (ring_send, ring_recv)
    pair = (pair_send, pair_recv)
    twins = [(twin_send.at[n], twin_recv.at[n]) for n in range(2)]

    def along_z(index):
        return {"slab": (slab + (2 if index < 2 else 14)) % 16}

    events = [(1, 0), (3, 2), (1, 1), (3, 3), (1, 2), (3, 0), (1, 3), (3, 1), (2, 0), (2, 2), (2, 1), (2, 3)]
    relays = {(1, 0): True, (1, 1): True, (3, 2): False, (3, 3): False}
    own_sends = [(1, 0, True), (3, 2, False), (1, 1, True), (3, 3, False)]
    own_sends += [(1, 2, True), (3, 0, False), (1, 3, True), (3, 1, False)]
    ring_sends = own_sends + [(2, event[1], way) for event, way in relays.items()]

    def on_ring(number):
        distance, index = events[number]
        moved(distance, index, parity, core, ring, at_x(1)).wait_recv()
        if events[number] in relays:
            ring_copy(2, index, relays[events[number]]).start()
        moved(distance, index, parity, core, pair, along_z(index)).start()
        moved(distance, index, parity, core, twins[0], {"slab": twin}).start()

    def on_pair(number):
        distance, index = events[number]
        moved(distance, index, 1 - parity, core, pair, along_z(index)).wait_recv()
        moved(distance, index, 1 - parity, core, twins[1], {"slab": twin}).start()

    for distance, index, from_left in own_sends:
        ring_copy(distance, index, from_left).start()

    def clip_copy(step):
        to = (slab + step) % 16
        return remote(
            staged.at[to], clip.at[slab], clip_send.at[step], clip_recv.at[step], {"slab": to}
        )

    def clip_arrival(step):
        return remote(
            staged.at[slab],
            clip.at[(slab + 16 - step) % 16],
            clip_send.at[step],
            clip_recv.at[step],
            {"slab": (slab + step) % 16},
        )

    @pl.loop(1, 16)
    def _(step):
        clip_copy(step).start()

    def norm_copy(step, owner):
        return remote(
            norms.at[owner], norms.at[owner], norm_send.at[step], norm_recv.at[step], at_x(step)
        )

    @pl.loop(1, SIDE)
    def _(step):
        norm_copy(step, x).start()

    clip[slab] = staged[slab]

    @pl.loop(0, 27)
    def _(tap):
        encoder_load(tap).wait()

    for number in range(4):
        on_ring(number)

    @pl.loop(1, 16)
    def _(step):
        clip_arrival(step).wait_recv()

    latent = encode(
        clip[...].reshape(512, 256),
        vae_gain[...],
        vae_shift[...],
        vae_bias[...],
        encoder,
        latent_weight[...],
        latent_bias[...],
    )
    offset = offsets[section, slots[section, slab]]
    first_state[:, 0:320] = embed(
        latent, offset, in_weight, in_bias[...].reshape(1, 320), table[...]
    )

    def first_copy():
        return remote(
            first_state, arriving.at[y], first_send, state_recv.at[y], {"section": x}
        )

    @pl.when(y == 0)
    def _():
        arriving[0] = first_state[...]

    @pl.when(y > 0)
    def _():
        first_copy().start()

    for number in range(4, 12):
        on_ring(number)
        on_pair(number - 4)
    for number in range(8, 12):
        on_pair(number)

    @pl.loop(1, SIDE)
    def _(step):
        norm_copy(step, (x + SIDE - step) % SIDE).wait_recv()

    for distance, index in events:
        for n in range(2):
            side = parity if n == 0 else 1 - parity
            moved(distance, index, side, 1 - core, twins[n], {"slab": twin}).wait_recv()

    def state_copy(turn):
        return remote(
            leaving.at[turn],
            arriving.at[turn],
            state_send.at[turn],
            state_recv.at[turn],
            {"section": (section + SIDE) % 16},
        )

    def out_copy(index):
        turn, layer = index // SIDE, index % SIDE
        micro = turn * SIDE + x
        return remote(
            results.at[index],
            out.at[micro],
            out_send.at[index],
            out_recv.at[micro],
            {"section": y * SIDE + layer},
        )

    def out_arrival(micro):
        return remote(
            results.at[micro],
            out.at[micro],
            out_send.at[micro],
            out_recv.at[micro],
            {"section": y * SIDE + micro % SIDE},
        )

    def keep_copy(turn):
        index = turn * SIDE + x
        return pltpu.make_async_copy(results.at[index], out.at[index], keep_sem.at[turn])

    @pl.loop(0, 16)
    def _(index):
        turn, layer = index // SIDE, index % SIDE

        @pl.when(jnp.logical_and(layer == 0, turn + y > 0))
        def _():
            state_copy(turn).wait_recv()

        @pl.when(layer == 0)
        def _():
            state[...] = arriving[turn].astype(F32).reshape(16, 8, 384)

        result = block(
            state[...],
            norms[layer, 0:1, :],
            norms[layer, 1:2, :],
            norms[layer, 2:3, :],
            packed.at[layer],
            members[...],
        )

        @pl.when(jnp.logical_and(layer == SIDE - 1, y < SIDE - 1))
        def _():
            leaving[turn] = result.reshape(128, 384)
            state_copy(turn).start()

        result = result.astype(F32)
        state[...] = result
        for n in range(3):
            spread[n] = result[:, :, n * 128 : (n + 1) * 128].reshape(128, 128)
        cells = []
        for col in range(4):
            every = pl.ds(col, 32, stride=4)
            cells += [spread[0, every, :], spread[1, every, :], spread[2, every, :][:, :64]]
        results[index] = jnp.concatenate(cells, axis=1).astype(BF)

        @pl.when(layer == x)
        def _():
            keep_copy(turn).start()

        @pl.when(layer != x)
        def _():
            out_copy(index).start()

    @pl.loop(0, 16)
    def _(index):
        @pl.when(index % SIDE != x)
        def _():
            out_copy(index).wait_send()
            out_arrival(index).wait_recv()

    @pl.loop(0, SIDE)
    def _(turn):
        keep_copy(turn).wait()

        @pl.when(y < SIDE - 1)
        def _():
            state_copy(turn).wait_send()

    @pl.when(y > 0)
    def _():
        first_copy().wait_send()

    @pl.loop(1, 16)
    def _(step):
        clip_copy(step).wait_send()

    @pl.loop(1, SIDE)
    def _(step):
        norm_copy(step, x).wait_send()

    for distance, index, from_left in ring_sends:
        ring_copy(distance, index, from_left).wait_send()
    for distance, index in events:
        moved(distance, index, parity, core, pair, along_z(index)).wait_send()
        for n in range(2):
            side = parity if n == 0 else 1 - parity
            moved(distance, index, side, core, twins[n], {"slab": twin}).wait_send()


def per_device(
    features,
    vae_weight,
    vae_gain,
    vae_shift,
    vae_bias,
    latent_weight,
    latent_bias,
    slot_clips,
    row_offsets,
    in_weight,
    in_bias,
    pos_table,
    unet_gain,
    unet_shift,
    unet_weight,
    unet_bias,
):
    hbm = pl.BlockSpec(memory_space=pltpu.HBM)
    anywhere = pl.BlockSpec(memory_space=pl.ANY)
    dma = pltpu.SemaphoreType.DMA
    result = pl.pallas_call(
        kernel,
        out_shape=jax.ShapeDtypeStruct((16, 32, 1280), BF),
        in_specs=[hbm] * 16,
        out_specs=anywhere,
        scratch_shapes=[
            pltpu.SMEM((16, 16), jnp.int32),
            pltpu.SMEM((16, 16), jnp.int32),
            pltpu.VMEM((16, 32, 256), BF),
            pltpu.VMEM((1, 256), F32),
            pltpu.VMEM((1, 256), F32),
            pltpu.VMEM((1, 256), F32),
            pltpu.VMEM((16, 256), BF),
            pltpu.VMEM((1, 16), F32),
            pltpu.VMEM((9, 16, 320), BF),
            pltpu.VMEM((320,), F32),
            pltpu.VMEM((320, 128), BF),
            pltpu.VMEM((1, 320), F32),
            pltpu.VMEM((1, 320), F32),
            pltpu.VMEM((1, 320), F32),
            pltpu.VMEM((16, 32, 256), BF),
            pltpu.VMEM((16, 32, 256), BF),
            pltpu.VMEM((3, 2304, 256), BF),
            pltpu.VMEM((9, 320, 320), BF),
            pltpu.VMEM((SIDE, 1024, 1024), BF),
            pltpu.VMEM((SIDE, 8, 384), F32),
            pltpu.VMEM((128, 384), BF),
            pltpu.VMEM((SIDE, 128, 384), BF),
            pltpu.VMEM((SIDE, 128, 384), BF),
            pltpu.VMEM((16, 32, 1280), BF),
            pltpu.VMEM((16, 8, 384), F32),
            pltpu.VMEM((3, 128, 128), F32),
            pltpu.VMEM((384, 384), BF),
            dma((28,)),
            dma((14,)),
            dma((16,)),
            dma((16,)),
            dma((SIDE,)),
            dma((SIDE,)),
            dma((12,)),
            dma((12,)),
            dma((12,)),
            dma((12,)),
            dma((2, 12)),
            dma((2, 12)),
            dma,
            dma((SIDE,)),
            dma((SIDE,)),
            dma((16,)),
            dma((16,)),
            dma((SIDE,)),
        ],
        compiler_params=pltpu.CompilerParams(
            collective_id=0, has_side_effects=True, vmem_limit_bytes=63 * 1024 * 1024
        ),
    )(
        slot_clips,
        row_offsets,
        features.reshape(16, 32, 256),
        vae_weight.reshape(27, 256, 256),
        vae_gain.reshape(1, 256),
        vae_shift.reshape(1, 256),
        vae_bias.reshape(1, 256),
        latent_weight.T,
        latent_bias.reshape(1, 16),
        in_weight.reshape(9, 16, 320),
        in_bias,
        pos_table.T,
        unet_gain,
        unet_shift,
        unet_bias,
        unet_weight.reshape(9, 320, 320),
    )
    return result.reshape(1, 16, 1, 16, 2, 1280)


def solution(mesh):
    return jax.shard_map(
        per_device,
        mesh=mesh,
        in_specs=(
            P("section", None, "slab", None, None, None),
            P(),
            P(),
            P(),
            P(),
            P(),
            P(),
            P(),
            P(),
            P(),
            P(),
            P(),
            P("section", None),
            P("section", None),
            P("section", None, None, None, None),
            P("section", None),
        ),
        out_specs=P("section", None, "slab", None, None, None),
        check_vma=False,
    )
```

```python
import jax
import jax.numpy as jnp
from jax import lax
from jax.experimental import pallas as pl
from jax.experimental.pallas import tpu as pltpu
from jax.sharding import PartitionSpec as P

BF = jnp.bfloat16
F32 = jnp.float32
MESH = pl.DeviceIdType.MESH
EPS = 1e-6
SIDE = 4
QUARTER = 240
CHUNKS = ((0, 64), (64, 64), (128, 64), (192, 48))


def group_matrix(used, width, group):
    a = lax.broadcasted_iota(jnp.int32, (width, width), 0)
    b = lax.broadcasted_iota(jnp.int32, (width, width), 1)
    same = (b - b % group) == (a - a % group)
    hit = jnp.logical_and(same, jnp.logical_and(a < used, b < used))
    return jnp.where(hit, 1.0, 0.0).astype(BF)


def partial_sums(values):
    return jnp.sum(values, axis=0), jnp.sum(values * values, axis=0)


def group_stats(partial, members, count):
    parts = []
    for eighths in partial:
        total = jnp.sum(eighths, axis=0, keepdims=True)
        high = total.astype(BF).astype(F32)
        rest = total - high
        mid = rest.astype(BF).astype(F32)
        parts += [high, mid, rest - mid]
    left = jnp.zeros_like(partial[0])
    row = lax.broadcasted_iota(jnp.int32, left.shape, 0)
    for index, part in enumerate(parts):
        left = jnp.where(row == index, part, left)
    sums = jnp.dot(left.astype(BF), members, preferred_element_type=F32)
    mean = (sums[0:1] + sums[1:2] + sums[2:3]) * (1.0 / count)
    meansq = (sums[3:4] + sums[4:5] + sums[5:6]) * (1.0 / count)
    return mean, lax.rsqrt(meansq - mean * mean + EPS)


def silu(v):
    half = 0.5 * v
    return half + half * jnp.tanh(half)


def across(left, right):
    return lax.dot_general(left, right, (((1,), (1,)), ((), ())), preferred_element_type=F32)


def up_down(values):
    zero = jnp.zeros_like(values[:1])
    return (
        jnp.concatenate([zero, values[:-1]], axis=0),
        jnp.concatenate([values[1:], zero], axis=0),
    )


def beside(values, step, cols):
    col = lax.broadcasted_iota(jnp.int32, values.shape, 1) % cols
    edge = 0 if step == 1 else cols - 1
    return jnp.where(col == edge, 0.0, pltpu.roll(values, step % 8, 1))


def block(y, stats, gain, shift, bias, weight):
    mean, inverse = stats
    act = silu((y - mean) * (inverse * gain) + shift)
    above, below = (a.reshape(128, 384) for a in up_down(act))
    here = act.reshape(128, 384)
    low = lax.broadcasted_iota(jnp.int32, (128, 128), 1) < 64
    tail = jnp.where(low, above[:, 256:], pltpu.roll(here[:, 256:], 64, 1))
    pieces = (above[:, :256], here[:, :256], below[:, :256], tail, below[:, 256:])
    left = jnp.concatenate([a.astype(BF) for a in pieces], axis=1)

    def product(n):
        return jnp.dot(left, weight[:, n * 256 : (n + 1) * 256], preferred_element_type=F32)

    def summed(before, middle, after, first, last):
        before, middle, after = (a.reshape(16, 8, last - first) for a in (before, middle, after))
        shifted = beside(before, 1, 4) + beside(after, -1, 4)
        return (y[:, :, first:last] + middle + shifted + bias[:, first:last]).astype(BF)

    tails = product(3)
    ends = tails[:, :128]
    high = summed(
        jnp.where(low, pltpu.roll(ends, 64, 1), 0.0),
        jnp.where(low, ends, 0.0),
        tails[:, 128:],
        256,
        384,
    )
    main = summed(product(0), product(1), product(2), 0, 256)
    return jnp.concatenate([main, high], axis=2)


def lay_out(y, spread):
    for n in range(3):
        spread[n] = y[:, :, n * 128 : (n + 1) * 128].reshape(128, 128)
    cells = []
    for col in range(4):
        every = pl.ds(col, 32, stride=4)
        cells += [spread[0, every, :], spread[1, every, :], spread[2, every, :][:, :64]]
    return jnp.concatenate(cells, axis=1).astype(BF).reshape(16, 2, 1280)


def pack_weight(raw, packed):
    packed[960:1024, :] = jnp.zeros((64, 1024), BF)
    for tap in range(3):
        for first, count, start in ((0, 256, tap * 256), (256, 64, 768 + 64 * tap)):
            rows = slice(start, start + count)
            ends = []
            for e in range(3):
                source = raw.at[tap * 3 + e]
                packed[rows, e * 256 : (e + 1) * 256] = source[first : first + count, :256]
                ends.append(source[first : first + count, 256:])
            packed[rows, 768:896] = jnp.concatenate([ends[1], ends[0]], axis=1)
            packed[rows, 896:1024] = jnp.concatenate([ends[2], jnp.zeros_like(ends[2])], axis=1)


def encode(clip, gain, shift, bias, weight, latent_weight, latent_bias):
    members = group_matrix(256, 256, 8)
    values = clip.astype(F32).reshape(64, 8, 256)
    mean, inverse = group_stats(partial_sums(values), members, 4096)
    act = silu((values - mean) * (inverse * gain) + shift).reshape(32, 2, 8, 256)
    lefts = []
    for frame in range(2):
        here = act[:, frame]
        above, below = up_down(here)
        lefts.append(
            jnp.concatenate([a.reshape(256, 256).astype(BF) for a in (above, here, below)], axis=1)
        )
    both = jnp.concatenate(lefts, axis=0)
    sums = [jnp.zeros((32, 8, 256), F32)] * 2
    for e in range(3):
        shared = jnp.dot(
            lefts[0], weight[e, 0:768, :], preferred_element_type=F32
        ) + jnp.dot(lefts[0], weight[e, 768:1536, :], preferred_element_type=F32)
        own = jnp.dot(both, weight[e, 1536:2304, :], preferred_element_type=F32)
        for frame in range(2):
            part = (shared + own[frame * 256 : (frame + 1) * 256]).reshape(32, 8, 256)
            sums[frame] = sums[frame] + (part if e == 1 else beside(part, 1 - e, 8))
    values = values.reshape(32, 2, 8, 256)
    paired = []
    for frame in range(2):
        summed = (values[:, frame] + sums[frame] + bias).reshape(16, 2, 8, 256)
        paired.append(summed[:, 0] + summed[:, 1])
    stacked = jnp.stack(paired, axis=1).reshape(256, 256)
    terms = []
    for _ in range(3):
        high = stacked.astype(BF)
        terms.append(high)
        stacked = stacked - high.astype(F32)
    row = lax.broadcasted_iota(jnp.int32, (128, 256), 0)
    col = lax.broadcasted_iota(jnp.int32, (128, 256), 1)
    pick = jnp.where(col - col % 2 == 2 * row, 1.0, 0.0).astype(BF)
    total = jnp.zeros((128, 256), F32)
    for high in terms:
        total = total + jnp.dot(pick, high, preferred_element_type=F32)
    pooled = (0.25 * total).astype(BF)
    latent = across(pooled, latent_weight) + latent_bias
    return latent.astype(BF).astype(F32)


def embed(latent, offset, weight, bias, table):
    grid = latent.reshape(16, 8, 16)
    columns = (beside(grid, 1, 4), grid, beside(grid, -1, 4))
    total = jnp.zeros((128, 320), F32)
    for e in range(3):
        above, below = up_down(columns[e])
        for b, rows in enumerate((above, columns[e], below)):
            total = total + jnp.dot(
                rows.reshape(128, 16).astype(BF), weight[b * 3 + e], preferred_element_type=F32
            )
    row = lax.broadcasted_iota(jnp.int32, (16, 8, 128), 0)
    entry = lax.broadcasted_iota(jnp.int32, (16, 8, 128), 2)
    one_hot = jnp.where(entry == row + offset, 1.0, 0.0).reshape(128, 128).astype(BF)
    placed = across(one_hot, table)
    return (total + bias + placed).astype(BF)


def kernel(
    slots_in,
    offsets_in,
    features_in,
    vae_weight,
    vae_gain_in,
    vae_shift_in,
    vae_bias_in,
    latent_weight_in,
    latent_bias_in,
    in_weight_in,
    in_bias_in,
    table_in,
    gain_in,
    shift_in,
    bias_in,
    unet_weight,
    out,
    slots,
    offsets,
    features,
    vae_gain,
    vae_shift,
    vae_bias,
    latent_weight,
    latent_bias,
    in_weight,
    in_bias,
    table,
    gain,
    shift,
    bias,
    staged,
    clip,
    encoder,
    raw,
    packed,
    norms,
    first_state,
    arriving,
    leaving,
    results,
    kept,
    spread,
    members,
    load_sem,
    small_sem,
    clip_send,
    clip_recv,
    norm_send,
    norm_recv,
    ring_send,
    ring_recv,
    pair_send,
    pair_recv,
    twin_send,
    twin_recv,
    first_send,
    state_send,
    state_recv,
    out_send,
    out_recv,
    keep_sem,
):
    section = lax.axis_index("section")
    slab = lax.axis_index("slab")
    x, y = section % SIDE, section // SIDE
    core = slab % 2
    parity = (slab // 2) % 2
    twin = slab + 1 - 2 * core

    def at_x(step):
        return {"section": y * SIDE + (x + step + SIDE) % SIDE}

    def remote(source, target, send, recv, device):
        return pltpu.make_async_remote_copy(
            src_ref=source,
            dst_ref=target,
            send_sem=send,
            recv_sem=recv,
            device_id=device,
            device_id_type=MESH,
        )

    weight_load = pltpu.make_async_copy(unet_weight, raw, load_sem.at[27])
    small = [
        pltpu.make_async_copy(source, target, small_sem.at[index])
        for index, (source, target) in enumerate(
            (
                (slots_in, slots),
                (offsets_in, offsets),
                (features_in, features),
                (gain_in, gain),
                (shift_in, shift),
                (bias_in, bias),
                (vae_gain_in, vae_gain),
                (vae_shift_in, vae_shift),
                (vae_bias_in, vae_bias),
                (latent_weight_in, latent_weight),
                (latent_bias_in, latent_bias),
                (in_weight_in, in_weight),
                (in_bias_in, in_bias),
                (table_in, table),
            )
        )
    ]

    def encoder_load(tap):
        a, b, e = tap // 9, (tap // 3) % 3, tap % 3
        return pltpu.make_async_copy(
            vae_weight.at[tap],
            encoder.at[e, pl.ds(a * 768 + b * 256, 256), :],
            load_sem.at[tap],
        )

    barrier = pltpu.get_barrier_semaphore()

    def greet(device):
        pl.semaphore_signal(barrier, 1, device_id=device, device_id_type=MESH)

    weight_load.start()

    @pl.loop(1, SIDE)
    def _(step):
        greet(at_x(step))
        greet({"section": ((y + step) % SIDE) * SIDE + x})

    @pl.loop(1, 16)
    def _(step):
        greet({"slab": (slab + step) % 16})

    for copy in small:
        copy.start()

    @pl.loop(0, 27)
    def _(tap):
        encoder_load(tap).start()

    for layer in range(SIDE):
        packed[layer, 960:1024, :] = jnp.zeros((64, 1024), BF)
    weight_load.wait()
    pack_weight(raw, packed.at[x])
    pl.semaphore_wait(barrier, 21)

    def chunk(owner, side, which, index):
        first, count = CHUNKS[index]
        start = (side * 2 + which) * QUARTER + first
        return packed.at[owner, pl.ds(pl.multiple_of(start, 16), count), :]

    def ring_copy(distance, index, from_left):
        step = 1 if from_left else -1
        owner = (x + step - distance + 2 * SIDE) % SIDE
        mine = chunk(owner, parity, core, index)
        at = (distance - 1) * 4 + index
        return remote(mine, mine, ring_send.at[at], ring_recv.at[at], at_x(step))

    def moved(distance, index, side, which, sems, device):
        owner = (x - distance + SIDE) % SIDE
        mine = chunk(owner, side, which, index)
        at = (distance - 1) * 4 + index
        return remote(mine, mine, sems[0].at[at], sems[1].at[at], device)

    ring = (ring_send, ring_recv)
    pair = (pair_send, pair_recv)
    twins = [(twin_send.at[n], twin_recv.at[n]) for n in range(2)]

    def along_z(index):
        return {"slab": (slab + (2 if index < 2 else 14)) % 16}

    events = [(1, 0), (3, 2), (1, 1), (3, 3), (2, 0), (2, 2), (2, 1), (2, 3), (1, 2), (3, 0), (1, 3), (3, 1)]
    relays = {(1, 0): True, (1, 1): True, (3, 2): False, (3, 3): False}
    own_sends = [(1, 0, True), (3, 2, False), (1, 1, True), (3, 3, False)]
    own_sends += [(1, 2, True), (3, 0, False), (1, 3, True), (3, 1, False)]
    ring_sends = own_sends + [(2, event[1], way) for event, way in relays.items()]

    def on_ring(number):
        distance, index = events[number]
        moved(distance, index, parity, core, ring, at_x(1)).wait_recv()
        if events[number] in relays:
            ring_copy(2, index, relays[events[number]]).start()
        moved(distance, index, parity, core, pair, along_z(index)).start()
        moved(distance, index, parity, core, twins[0], {"slab": twin}).start()

    def on_pair(number):
        distance, index = events[number]
        moved(distance, index, 1 - parity, core, pair, along_z(index)).wait_recv()
        moved(distance, index, 1 - parity, core, twins[1], {"slab": twin}).start()

    for distance, index, from_left in own_sends[:4]:
        ring_copy(distance, index, from_left).start()

    for copy in small:
        copy.wait()

    @pl.loop(0, 16)
    def _(slot):
        staged[slot] = features[slots[section, slot]]


    def clip_copy(step):
        to = (slab + step) % 16
        return remote(
            staged.at[to], clip.at[slab], clip_send.at[step], clip_recv.at[step], {"slab": to}
        )

    def clip_arrival(step):
        return remote(
            staged.at[slab],
            clip.at[(slab + 16 - step) % 16],
            clip_send.at[step],
            clip_recv.at[step],
            {"slab": (slab + step) % 16},
        )

    @pl.loop(1, 16)
    def _(step):
        clip_copy(step).start()

    norms[x] = jnp.zeros((8, 384), F32)
    norms[x, 0:1, 0:320] = gain[...]
    norms[x, 1:2, 0:320] = shift[...]
    norms[x, 2:3, 0:320] = bias[...]

    def norm_copy(step, owner):
        return remote(
            norms.at[owner], norms.at[owner], norm_send.at[step], norm_recv.at[step], at_x(step)
        )

    @pl.loop(1, SIDE)
    def _(step):
        norm_copy(step, x).start()

    clip[slab] = staged[slab]
    members[...] = group_matrix(320, 384, 10)
    first_state[...] = jnp.zeros((128, 384), BF)

    @pl.loop(0, 27)
    def _(tap):
        encoder_load(tap).wait()

    for number in range(4):
        on_ring(number)
    for distance, index, from_left in own_sends[4:]:
        ring_copy(distance, index, from_left).start()

    @pl.loop(1, 16)
    def _(step):
        clip_arrival(step).wait_recv()

    latent = encode(
        clip[...].reshape(512, 256),
        vae_gain[...],
        vae_shift[...],
        vae_bias[...],
        encoder,
        latent_weight[...],
        latent_bias[...],
    )
    offset = offsets[section, slots[section, slab]]
    first_state[:, 0:320] = embed(
        latent, offset, in_weight, in_bias[...].reshape(1, 320), table[...]
    )

    def first_copy():
        return remote(
            first_state, arriving.at[y], first_send, state_recv.at[y], {"section": x}
        )

    @pl.when(y == 0)
    def _():
        arriving[0] = first_state[...]

    @pl.when(y > 0)
    def _():
        first_copy().start()

    for number in range(4, 12):
        on_ring(number)
        on_pair(number - 4)
    for number in range(8, 12):
        on_pair(number)

    @pl.loop(1, SIDE)
    def _(step):
        norm_copy(step, (x + SIDE - step) % SIDE).wait_recv()

    for distance, index in events:
        for n in range(2):
            side = parity if n == 0 else 1 - parity
            moved(distance, index, side, 1 - core, twins[n], {"slab": twin}).wait_recv()

    def state_copy(turn):
        return remote(
            leaving.at[turn],
            arriving.at[turn],
            state_send.at[turn],
            state_recv.at[turn],
            {"section": (section + SIDE) % 16},
        )

    def out_copy(index):
        turn, layer = index // SIDE, index % SIDE
        micro = turn * SIDE + x
        return remote(
            results.at[index],
            out.at[micro],
            out_send.at[index],
            out_recv.at[micro],
            {"section": y * SIDE + layer},
        )

    def out_arrival(micro):
        return remote(
            results.at[micro],
            out.at[micro],
            out_send.at[micro],
            out_recv.at[micro],
            {"section": y * SIDE + micro % SIDE},
        )

    def keep_copy(turn):
        index = turn * SIDE + x
        return pltpu.make_async_copy(results.at[index], out.at[index], keep_sem.at[turn])

    def push(turn, layer):
        @pl.when(layer == x)
        def _():
            keep_copy(turn).start()

        @pl.when(layer != x)
        def _():
            out_copy(turn * SIDE + layer).start()

    @pl.loop(0, SIDE)
    def _(turn):
        @pl.when(turn + y > 0)
        def _():
            state_copy(turn).wait_recv()

        state = arriving[turn].astype(F32).reshape(16, 8, 384)
        partial = partial_sums(state)
        for layer in range(SIDE):
            stats = group_stats(partial, members[...], 1280)
            if layer > 0:
                results[turn * SIDE + layer - 1] = lay_out(state, spread)
            result = block(
                state,
                stats,
                norms[layer, 0:1, :],
                norms[layer, 1:2, :],
                norms[layer, 2:3, :],
                packed.at[layer],
            )
            if layer == SIDE - 1:

                @pl.when(y < SIDE - 1)
                def _():
                    leaving[turn] = result.reshape(128, 384)
                    state_copy(turn).start()

            state = result.astype(F32)
            partial = partial_sums(state)
            kept[...] = state
            state = kept[...]
            if layer > 0:
                push(turn, layer - 1)
        results[turn * SIDE + SIDE - 1] = lay_out(state, spread)
        push(turn, SIDE - 1)

    @pl.loop(0, 16)
    def _(index):
        @pl.when(index % SIDE != x)
        def _():
            out_copy(index).wait_send()
            out_arrival(index).wait_recv()

    @pl.loop(0, SIDE)
    def _(turn):
        keep_copy(turn).wait()

        @pl.when(y < SIDE - 1)
        def _():
            state_copy(turn).wait_send()

    @pl.when(y > 0)
    def _():
        first_copy().wait_send()

    @pl.loop(1, 16)
    def _(step):
        clip_copy(step).wait_send()

    @pl.loop(1, SIDE)
    def _(step):
        norm_copy(step, x).wait_send()

    for distance, index, from_left in ring_sends:
        ring_copy(distance, index, from_left).wait_send()
    for distance, index in events:
        moved(distance, index, parity, core, pair, along_z(index)).wait_send()
        for n in range(2):
            side = parity if n == 0 else 1 - parity
            moved(distance, index, side, core, twins[n], {"slab": twin}).wait_send()


def hand_over(source, target, buffer, sems):
    loads = [pltpu.make_async_copy(source.at[m], buffer.at[m], sems.at[0, m]) for m in range(16)]
    stores = [pltpu.make_async_copy(buffer.at[m], target.at[m], sems.at[1, m]) for m in range(16)]
    for copy in loads:
        copy.start()
    for load, store in zip(loads, stores):
        load.wait()
        store.start()
    for copy in stores:
        copy.wait()


def per_device(
    features,
    vae_weight,
    vae_gain,
    vae_shift,
    vae_bias,
    latent_weight,
    latent_bias,
    slot_clips,
    row_offsets,
    in_weight,
    in_bias,
    pos_table,
    unet_gain,
    unet_shift,
    unet_weight,
    unet_bias,
):
    hbm = pl.BlockSpec(memory_space=pltpu.HBM)
    anywhere = pl.BlockSpec(memory_space=pl.ANY)
    dma = pltpu.SemaphoreType.DMA
    result = pl.pallas_call(
        kernel,
        out_shape=jax.ShapeDtypeStruct((16, 16, 2, 1280), BF),
        in_specs=[hbm] * 16,
        out_specs=anywhere,
        scratch_shapes=[
            pltpu.SMEM((16, 16), jnp.int32),
            pltpu.SMEM((16, 16), jnp.int32),
            pltpu.VMEM((16, 32, 256), BF),
            pltpu.VMEM((1, 256), F32),
            pltpu.VMEM((1, 256), F32),
            pltpu.VMEM((1, 256), F32),
            pltpu.VMEM((16, 256), BF),
            pltpu.VMEM((1, 16), F32),
            pltpu.VMEM((9, 16, 320), BF),
            pltpu.VMEM((320,), F32),
            pltpu.VMEM((320, 128), BF),
            pltpu.VMEM((1, 320), F32),
            pltpu.VMEM((1, 320), F32),
            pltpu.VMEM((1, 320), F32),
            pltpu.VMEM((16, 32, 256), BF),
            pltpu.VMEM((16, 32, 256), BF),
            pltpu.VMEM((3, 2304, 256), BF),
            pltpu.VMEM((9, 320, 320), BF),
            pltpu.VMEM((SIDE, 1024, 1024), BF),
            pltpu.VMEM((SIDE, 8, 384), F32),
            pltpu.VMEM((128, 384), BF),
            pltpu.VMEM((SIDE, 128, 384), BF),
            pltpu.VMEM((SIDE, 128, 384), BF),
            pltpu.VMEM((16, 16, 2, 1280), BF),
            pltpu.VMEM((16, 8, 384), F32),
            pltpu.VMEM((3, 128, 128), F32),
            pltpu.VMEM((384, 384), BF),
            dma((28,)),
            dma((14,)),
            dma((16,)),
            dma((16,)),
            dma((SIDE,)),
            dma((SIDE,)),
            dma((12,)),
            dma((12,)),
            dma((12,)),
            dma((12,)),
            dma((2, 12)),
            dma((2, 12)),
            dma,
            dma((SIDE,)),
            dma((SIDE,)),
            dma((16,)),
            dma((16,)),
            dma((SIDE,)),
        ],
        compiler_params=pltpu.CompilerParams(
            collective_id=0, has_side_effects=True, vmem_limit_bytes=63 * 1024 * 1024
        ),
    )(
        slot_clips,
        row_offsets,
        features.reshape(16, 32, 256),
        vae_weight.reshape(27, 256, 256),
        vae_gain.reshape(1, 256),
        vae_shift.reshape(1, 256),
        vae_bias.reshape(1, 256),
        latent_weight.T,
        latent_bias.reshape(1, 16),
        in_weight.reshape(9, 16, 320),
        in_bias,
        pos_table.T,
        unet_gain,
        unet_shift,
        unet_bias,
        unet_weight.reshape(9, 320, 320),
    )
    result = pl.pallas_call(
        hand_over,
        out_shape=jax.ShapeDtypeStruct((16, 16, 2, 1280), BF),
        in_specs=[hbm],
        out_specs=hbm,
        scratch_shapes=[pltpu.VMEM((16, 16, 2, 1280), BF), dma((2, 16))],
    )(result)
    return result.reshape(1, 16, 1, 16, 2, 1280)


def solution(mesh):
    return jax.shard_map(
        per_device,
        mesh=mesh,
        in_specs=(
            P("section", None, "slab", None, None, None),
            P(),
            P(),
            P(),
            P(),
            P(),
            P(),
            P(),
            P(),
            P(),
            P(),
            P(),
            P("section", None),
            P("section", None),
            P("section", None, None, None, None),
            P("section", None),
        ),
        out_specs=P("section", None, "slab", None, None, None),
        check_vma=False,
    )
```

```python
import jax
import jax.numpy as jnp
from jax import lax
from jax.experimental import pallas as pl
from jax.experimental.pallas import tpu as pltpu
from jax.sharding import PartitionSpec as P

BF = jnp.bfloat16
F32 = jnp.float32
MESH = pl.DeviceIdType.MESH
EPS = 1e-6
SIDE = 4
QUARTER = 240
CHUNKS = ((0, 64), (64, 64), (128, 64), (192, 48))


def group_matrix(used, width, group):
    a = lax.broadcasted_iota(jnp.int32, (width, width), 0)
    b = lax.broadcasted_iota(jnp.int32, (width, width), 1)
    same = (b - b % group) == (a - a % group)
    hit = jnp.logical_and(same, jnp.logical_and(a < used, b < used))
    return jnp.where(hit, 1.0, 0.0).astype(BF)


def partial_sums(values):
    return jnp.sum(values, axis=0), jnp.sum(values * values, axis=0)


def group_stats(partial, members, count):
    parts = []
    for eighths in partial:
        total = jnp.sum(eighths, axis=0, keepdims=True)
        high = total.astype(BF).astype(F32)
        rest = total - high
        mid = rest.astype(BF).astype(F32)
        parts += [high, mid, rest - mid]
    left = jnp.zeros_like(partial[0])
    row = lax.broadcasted_iota(jnp.int32, left.shape, 0)
    for index, part in enumerate(parts):
        left = jnp.where(row == index, part, left)
    sums = jnp.dot(left.astype(BF), members, preferred_element_type=F32)
    mean = (sums[0:1] + sums[1:2] + sums[2:3]) * (1.0 / count)
    meansq = (sums[3:4] + sums[4:5] + sums[5:6]) * (1.0 / count)
    return mean, lax.rsqrt(meansq - mean * mean + EPS)


def silu(v):
    half = 0.5 * v
    return half + half * jnp.tanh(half)


def across(left, right):
    return lax.dot_general(left, right, (((1,), (1,)), ((), ())), preferred_element_type=F32)


def up_down(values):
    zero = jnp.zeros_like(values[:1])
    return (
        jnp.concatenate([zero, values[:-1]], axis=0),
        jnp.concatenate([values[1:], zero], axis=0),
    )


def beside(values, step, cols):
    col = lax.broadcasted_iota(jnp.int32, values.shape, 1) % cols
    edge = 0 if step == 1 else cols - 1
    return jnp.where(col == edge, 0.0, pltpu.roll(values, step % 8, 1))


def block(y, stats, gain, shift, bias, weight):
    mean, inverse = stats
    act = silu((y - mean) * (inverse * gain) + shift)
    above, below = (a.reshape(128, 384) for a in up_down(act))
    here = act.reshape(128, 384)
    low = lax.broadcasted_iota(jnp.int32, (128, 128), 1) < 64
    tail = jnp.where(low, above[:, 256:], pltpu.roll(here[:, 256:], 64, 1))
    pieces = (above[:, :256], here[:, :256], below[:, :256], tail, below[:, 256:])
    left = jnp.concatenate([a.astype(BF) for a in pieces], axis=1)

    def product(n):
        return jnp.dot(left, weight[:, n * 256 : (n + 1) * 256], preferred_element_type=F32)

    def summed(before, middle, after, first, last):
        before, middle, after = (a.reshape(16, 8, last - first) for a in (before, middle, after))
        shifted = beside(before, 1, 4) + beside(after, -1, 4)
        return (y[:, :, first:last] + middle + shifted + bias[:, first:last]).astype(BF)

    tails = product(3)
    ends = tails[:, :128]
    high = summed(
        jnp.where(low, pltpu.roll(ends, 64, 1), 0.0),
        jnp.where(low, ends, 0.0),
        tails[:, 128:],
        256,
        384,
    )
    main = summed(product(0), product(1), product(2), 0, 256)
    return jnp.concatenate([main, high], axis=2)


def lay_out(y, spread):
    for n in range(3):
        spread[n] = y[:, :, n * 128 : (n + 1) * 128].reshape(128, 128)
    cells = []
    for col in range(4):
        every = pl.ds(col, 32, stride=4)
        cells += [spread[0, every, :], spread[1, every, :], spread[2, every, :][:, :64]]
    return jnp.concatenate(cells, axis=1).astype(BF).reshape(16, 2, 1280)


def fold(y, target):
    ends = y[:, 256:320]
    target[0:128, :] = y[:, :128].astype(BF)
    target[128:256, :] = y[:, 128:256].astype(BF)
    target[256:320, :] = jnp.concatenate([ends[:64], ends[64:]], axis=1).astype(BF)


def unfold(source):
    ends = source[256:320, :].astype(F32)
    low = lax.broadcasted_iota(jnp.int32, (64, 128), 1) < 64
    tops = jnp.where(low, ends, 0.0)
    bottoms = jnp.where(low, pltpu.roll(ends, 64, 1), 0.0)
    parts = (
        source[0:128, :].astype(F32),
        source[128:256, :].astype(F32),
        jnp.concatenate([tops, bottoms], axis=0),
    )
    return jnp.concatenate(parts, axis=1).reshape(16, 8, 384)


def pack_weight(raw, packed):
    packed[960:1024, :] = jnp.zeros((64, 1024), BF)
    for tap in range(3):
        for first, count, start in ((0, 256, tap * 256), (256, 64, 768 + 64 * tap)):
            rows = slice(start, start + count)
            ends = []
            for e in range(3):
                source = raw.at[tap * 3 + e]
                packed[rows, e * 256 : (e + 1) * 256] = source[first : first + count, :256]
                ends.append(source[first : first + count, 256:])
            packed[rows, 768:896] = jnp.concatenate([ends[1], ends[0]], axis=1)
            packed[rows, 896:1024] = jnp.concatenate([ends[2], jnp.zeros_like(ends[2])], axis=1)


def encode(clip, gain, shift, bias, weight, latent_weight, latent_bias):
    members = group_matrix(256, 256, 8)
    values = clip.astype(F32).reshape(64, 8, 256)
    mean, inverse = group_stats(partial_sums(values), members, 4096)
    act = silu((values - mean) * (inverse * gain) + shift).reshape(32, 2, 8, 256)
    lefts = []
    for frame in range(2):
        here = act[:, frame]
        above, below = up_down(here)
        lefts.append(
            jnp.concatenate([a.reshape(256, 256).astype(BF) for a in (above, here, below)], axis=1)
        )
    both = jnp.concatenate(lefts, axis=0)
    sums = [jnp.zeros((32, 8, 256), F32)] * 2
    for e in range(3):
        shared = jnp.dot(
            lefts[0], weight[e, 0:768, :], preferred_element_type=F32
        ) + jnp.dot(lefts[0], weight[e, 768:1536, :], preferred_element_type=F32)
        own = jnp.dot(both, weight[e, 1536:2304, :], preferred_element_type=F32)
        for frame in range(2):
            part = (shared + own[frame * 256 : (frame + 1) * 256]).reshape(32, 8, 256)
            sums[frame] = sums[frame] + (part if e == 1 else beside(part, 1 - e, 8))
    values = values.reshape(32, 2, 8, 256)
    paired = []
    for frame in range(2):
        summed = (values[:, frame] + sums[frame] + bias).reshape(16, 2, 8, 256)
        paired.append(summed[:, 0] + summed[:, 1])
    stacked = jnp.stack(paired, axis=1).reshape(256, 256)
    terms = []
    for _ in range(3):
        high = stacked.astype(BF)
        terms.append(high)
        stacked = stacked - high.astype(F32)
    row = lax.broadcasted_iota(jnp.int32, (128, 256), 0)
    col = lax.broadcasted_iota(jnp.int32, (128, 256), 1)
    pick = jnp.where(col - col % 2 == 2 * row, 1.0, 0.0).astype(BF)
    total = jnp.zeros((128, 256), F32)
    for high in terms:
        total = total + jnp.dot(pick, high, preferred_element_type=F32)
    pooled = (0.25 * total).astype(BF)
    latent = across(pooled, latent_weight) + latent_bias
    return latent.astype(BF).astype(F32)


def embed(latent, offset, weight, bias, table):
    grid = latent.reshape(16, 8, 16)
    columns = (beside(grid, 1, 4), grid, beside(grid, -1, 4))
    total = jnp.zeros((128, 320), F32)
    for e in range(3):
        above, below = up_down(columns[e])
        for b, rows in enumerate((above, columns[e], below)):
            total = total + jnp.dot(
                rows.reshape(128, 16).astype(BF), weight[b * 3 + e], preferred_element_type=F32
            )
    row = lax.broadcasted_iota(jnp.int32, (16, 8, 128), 0)
    entry = lax.broadcasted_iota(jnp.int32, (16, 8, 128), 2)
    one_hot = jnp.where(entry == row + offset, 1.0, 0.0).reshape(128, 128).astype(BF)
    placed = across(one_hot, table)
    return total + bias + placed


def kernel(
    slots_in,
    offsets_in,
    features_in,
    vae_weight,
    vae_gain_in,
    vae_shift_in,
    vae_bias_in,
    latent_weight_in,
    latent_bias_in,
    in_weight_in,
    in_bias_in,
    table_in,
    gain_in,
    shift_in,
    bias_in,
    unet_weight,
    out,
    slots,
    offsets,
    features,
    vae_gain,
    vae_shift,
    vae_bias,
    latent_weight,
    latent_bias,
    in_weight,
    in_bias,
    table,
    gain,
    shift,
    bias,
    staged,
    clip,
    encoder,
    raw,
    packed,
    norms,
    first_state,
    arriving,
    leaving,
    results,
    kept,
    spread,
    members,
    load_sem,
    small_sem,
    clip_send,
    clip_recv,
    norm_send,
    norm_recv,
    ring_send,
    ring_recv,
    pair_send,
    pair_recv,
    twin_send,
    twin_recv,
    first_send,
    state_send,
    state_recv,
    out_send,
    out_recv,
    keep_sem,
):
    section = lax.axis_index("section")
    slab = lax.axis_index("slab")
    x, y = section % SIDE, section // SIDE
    core = slab % 2
    parity = (slab // 2) % 2
    twin = slab + 1 - 2 * core

    def at_x(step):
        return {"section": y * SIDE + (x + step + SIDE) % SIDE}

    def remote(source, target, send, recv, device):
        return pltpu.make_async_remote_copy(
            src_ref=source,
            dst_ref=target,
            send_sem=send,
            recv_sem=recv,
            device_id=device,
            device_id_type=MESH,
        )

    weight_load = pltpu.make_async_copy(unet_weight, raw, load_sem.at[27])
    small = [
        pltpu.make_async_copy(source, target, small_sem.at[index])
        for index, (source, target) in enumerate(
            (
                (slots_in, slots),
                (offsets_in, offsets),
                (features_in, features),
                (gain_in, gain),
                (shift_in, shift),
                (bias_in, bias),
                (vae_gain_in, vae_gain),
                (vae_shift_in, vae_shift),
                (vae_bias_in, vae_bias),
                (latent_weight_in, latent_weight),
                (latent_bias_in, latent_bias),
                (in_weight_in, in_weight),
                (in_bias_in, in_bias),
                (table_in, table),
            )
        )
    ]

    def encoder_load(tap):
        a, b, e = tap // 9, (tap // 3) % 3, tap % 3
        return pltpu.make_async_copy(
            vae_weight.at[tap],
            encoder.at[e, pl.ds(a * 768 + b * 256, 256), :],
            load_sem.at[tap],
        )

    barrier = pltpu.get_barrier_semaphore()

    def greet(device):
        pl.semaphore_signal(barrier, 1, device_id=device, device_id_type=MESH)

    weight_load.start()

    @pl.loop(1, SIDE)
    def _(step):
        greet(at_x(step))
        greet({"section": ((y + step) % SIDE) * SIDE + x})

    @pl.loop(1, 16)
    def _(step):
        greet({"slab": (slab + step) % 16})

    for copy in small:
        copy.start()

    @pl.loop(0, 27)
    def _(tap):
        encoder_load(tap).start()

    for layer in range(SIDE):
        packed[layer, 960:1024, :] = jnp.zeros((64, 1024), BF)
    weight_load.wait()
    pack_weight(raw, packed.at[x])
    pl.semaphore_wait(barrier, 21)

    def chunk(owner, side, which, index):
        first, count = CHUNKS[index]
        start = (side * 2 + which) * QUARTER + first
        return packed.at[owner, pl.ds(pl.multiple_of(start, 16), count), :]

    def ring_copy(distance, index, from_left):
        step = 1 if from_left else -1
        owner = (x + step - distance + 2 * SIDE) % SIDE
        mine = chunk(owner, parity, core, index)
        at = (distance - 1) * 4 + index
        return remote(mine, mine, ring_send.at[at], ring_recv.at[at], at_x(step))

    def moved(distance, index, side, which, sems, device):
        owner = (x - distance + SIDE) % SIDE
        mine = chunk(owner, side, which, index)
        at = (distance - 1) * 4 + index
        return remote(mine, mine, sems[0].at[at], sems[1].at[at], device)

    ring = (ring_send, ring_recv)
    pair = (pair_send, pair_recv)
    twins = [(twin_send.at[n], twin_recv.at[n]) for n in range(2)]

    def along_z(index):
        return {"slab": (slab + (2 if index < 2 else 14)) % 16}

    events = [(1, 0), (3, 2), (1, 1), (3, 3), (2, 0), (2, 2), (2, 1), (2, 3), (1, 2), (3, 0), (1, 3), (3, 1)]
    relays = {(1, 0): True, (1, 1): True, (3, 2): False, (3, 3): False}
    own_sends = [(1, 0, True), (3, 2, False), (1, 1, True), (3, 3, False)]
    own_sends += [(1, 2, True), (3, 0, False), (1, 3, True), (3, 1, False)]
    ring_sends = own_sends + [(2, event[1], way) for event, way in relays.items()]

    def on_ring(number):
        distance, index = events[number]
        moved(distance, index, parity, core, ring, at_x(1)).wait_recv()
        if events[number] in relays:
            ring_copy(2, index, relays[events[number]]).start()
        moved(distance, index, parity, core, pair, along_z(index)).start()
        moved(distance, index, parity, core, twins[0], {"slab": twin}).start()

    def on_pair(number):
        distance, index = events[number]
        moved(distance, index, 1 - parity, core, pair, along_z(index)).wait_recv()
        moved(distance, index, 1 - parity, core, twins[1], {"slab": twin}).start()

    for distance, index, from_left in own_sends[:4]:
        ring_copy(distance, index, from_left).start()

    for copy in small:
        copy.wait()

    @pl.loop(0, 16)
    def _(slot):
        staged[slot] = features[slots[section, slot]]


    def clip_copy(step):
        to = (slab + step) % 16
        return remote(
            staged.at[to], clip.at[slab], clip_send.at[step], clip_recv.at[step], {"slab": to}
        )

    def clip_arrival(step):
        return remote(
            staged.at[slab],
            clip.at[(slab + 16 - step) % 16],
            clip_send.at[step],
            clip_recv.at[step],
            {"slab": (slab + step) % 16},
        )

    @pl.loop(1, 16)
    def _(step):
        clip_copy(step).start()

    norms[x] = jnp.zeros((8, 384), F32)
    norms[x, 0:1, 0:320] = gain[...]
    norms[x, 1:2, 0:320] = shift[...]
    norms[x, 2:3, 0:320] = bias[...]

    def norm_copy(step, owner):
        return remote(
            norms.at[owner], norms.at[owner], norm_send.at[step], norm_recv.at[step], at_x(step)
        )

    @pl.loop(1, SIDE)
    def _(step):
        norm_copy(step, x).start()

    clip[slab] = staged[slab]
    members[...] = group_matrix(320, 384, 10)

    @pl.loop(0, 27)
    def _(tap):
        encoder_load(tap).wait()

    for number in range(4):
        on_ring(number)
    for distance, index, from_left in own_sends[4:]:
        ring_copy(distance, index, from_left).start()

    @pl.loop(1, 16)
    def _(step):
        clip_arrival(step).wait_recv()

    latent = encode(
        clip[...].reshape(512, 256),
        vae_gain[...],
        vae_shift[...],
        vae_bias[...],
        encoder,
        latent_weight[...],
        latent_bias[...],
    )
    offset = offsets[section, slots[section, slab]]
    embedded = embed(latent, offset, in_weight, in_bias[...].reshape(1, 320), table[...])
    fold(embedded, first_state)

    def first_copy():
        return remote(
            first_state, arriving.at[y], first_send, state_recv.at[y], {"section": x}
        )

    @pl.when(y == 0)
    def _():
        arriving[0] = first_state[...]

    @pl.when(y > 0)
    def _():
        first_copy().start()

    for number in range(4, 12):
        on_ring(number)
        on_pair(number - 4)
    for number in range(8, 12):
        on_pair(number)

    @pl.loop(1, SIDE)
    def _(step):
        norm_copy(step, (x + SIDE - step) % SIDE).wait_recv()

    for distance, index in events:
        for n in range(2):
            side = parity if n == 0 else 1 - parity
            moved(distance, index, side, 1 - core, twins[n], {"slab": twin}).wait_recv()

    def state_copy(turn):
        return remote(
            leaving.at[turn],
            arriving.at[turn],
            state_send.at[turn],
            state_recv.at[turn],
            {"section": (section + SIDE) % 16},
        )

    def out_copy(index):
        turn, layer = index // SIDE, index % SIDE
        micro = turn * SIDE + x
        return remote(
            results.at[index],
            out.at[micro],
            out_send.at[index],
            out_recv.at[micro],
            {"section": y * SIDE + layer},
        )

    def out_arrival(micro):
        return remote(
            results.at[micro],
            out.at[micro],
            out_send.at[micro],
            out_recv.at[micro],
            {"section": y * SIDE + micro % SIDE},
        )

    def keep_copy(turn):
        index = turn * SIDE + x
        return pltpu.make_async_copy(results.at[index], out.at[index], keep_sem.at[turn])

    def push(turn, layer):
        @pl.when(layer == x)
        def _():
            keep_copy(turn).start()

        @pl.when(layer != x)
        def _():
            out_copy(turn * SIDE + layer).start()

    @pl.loop(0, SIDE)
    def _(turn):
        @pl.when(turn + y > 0)
        def _():
            state_copy(turn).wait_recv()

        state = unfold(arriving.at[turn])
        partial = partial_sums(state)
        for layer in range(SIDE):
            stats = group_stats(partial, members[...], 1280)
            if layer > 0:
                results[turn * SIDE + layer - 1] = lay_out(state, spread)
            result = block(
                state,
                stats,
                norms[layer, 0:1, :],
                norms[layer, 1:2, :],
                norms[layer, 2:3, :],
                packed.at[layer],
            )
            if layer == SIDE - 1:

                @pl.when(y < SIDE - 1)
                def _():
                    fold(result.astype(F32).reshape(128, 384), leaving.at[turn])
                    state_copy(turn).start()

            state = result.astype(F32)
            partial = partial_sums(state)
            kept[...] = state
            state = kept[...]
            if layer > 0:
                push(turn, layer - 1)
        results[turn * SIDE + SIDE - 1] = lay_out(state, spread)
        push(turn, SIDE - 1)

    @pl.loop(0, 16)
    def _(index):
        @pl.when(index % SIDE != x)
        def _():
            out_copy(index).wait_send()
            out_arrival(index).wait_recv()

    @pl.loop(0, SIDE)
    def _(turn):
        keep_copy(turn).wait()

        @pl.when(y < SIDE - 1)
        def _():
            state_copy(turn).wait_send()

    @pl.when(y > 0)
    def _():
        first_copy().wait_send()

    @pl.loop(1, 16)
    def _(step):
        clip_copy(step).wait_send()

    @pl.loop(1, SIDE)
    def _(step):
        norm_copy(step, x).wait_send()

    for distance, index, from_left in ring_sends:
        ring_copy(distance, index, from_left).wait_send()
    for distance, index in events:
        moved(distance, index, parity, core, pair, along_z(index)).wait_send()
        for n in range(2):
            side = parity if n == 0 else 1 - parity
            moved(distance, index, side, core, twins[n], {"slab": twin}).wait_send()


def hand_over(source, target, buffer, sems):
    parts = [pl.ds(n * 4, 4) for n in range(4)]
    loads = [pltpu.make_async_copy(source.at[p], buffer.at[p], sems.at[0, n]) for n, p in enumerate(parts)]
    stores = [pltpu.make_async_copy(buffer.at[p], target.at[p], sems.at[1, n]) for n, p in enumerate(parts)]
    for copy in loads:
        copy.start()
    for load, store in zip(loads, stores):
        load.wait()
        store.start()
    for copy in stores:
        copy.wait()


def per_device(
    features,
    vae_weight,
    vae_gain,
    vae_shift,
    vae_bias,
    latent_weight,
    latent_bias,
    slot_clips,
    row_offsets,
    in_weight,
    in_bias,
    pos_table,
    unet_gain,
    unet_shift,
    unet_weight,
    unet_bias,
):
    hbm = pl.BlockSpec(memory_space=pltpu.HBM)
    anywhere = pl.BlockSpec(memory_space=pl.ANY)
    dma = pltpu.SemaphoreType.DMA
    result = pl.pallas_call(
        kernel,
        out_shape=jax.ShapeDtypeStruct((16, 16, 2, 1280), BF),
        in_specs=[hbm] * 16,
        out_specs=anywhere,
        scratch_shapes=[
            pltpu.SMEM((16, 16), jnp.int32),
            pltpu.SMEM((16, 16), jnp.int32),
            pltpu.VMEM((16, 32, 256), BF),
            pltpu.VMEM((1, 256), F32),
            pltpu.VMEM((1, 256), F32),
            pltpu.VMEM((1, 256), F32),
            pltpu.VMEM((16, 256), BF),
            pltpu.VMEM((1, 16), F32),
            pltpu.VMEM((9, 16, 320), BF),
            pltpu.VMEM((320,), F32),
            pltpu.VMEM((320, 128), BF),
            pltpu.VMEM((1, 320), F32),
            pltpu.VMEM((1, 320), F32),
            pltpu.VMEM((1, 320), F32),
            pltpu.VMEM((16, 32, 256), BF),
            pltpu.VMEM((16, 32, 256), BF),
            pltpu.VMEM((3, 2304, 256), BF),
            pltpu.VMEM((9, 320, 320), BF),
            pltpu.VMEM((SIDE, 1024, 1024), BF),
            pltpu.VMEM((SIDE, 8, 384), F32),
            pltpu.VMEM((320, 128), BF),
            pltpu.VMEM((SIDE, 320, 128), BF),
            pltpu.VMEM((SIDE, 320, 128), BF),
            pltpu.VMEM((16, 16, 2, 1280), BF),
            pltpu.VMEM((16, 8, 384), F32),
            pltpu.VMEM((3, 128, 128), F32),
            pltpu.VMEM((384, 384), BF),
            dma((28,)),
            dma((14,)),
            dma((16,)),
            dma((16,)),
            dma((SIDE,)),
            dma((SIDE,)),
            dma((12,)),
            dma((12,)),
            dma((12,)),
            dma((12,)),
            dma((2, 12)),
            dma((2, 12)),
            dma,
            dma((SIDE,)),
            dma((SIDE,)),
            dma((16,)),
            dma((16,)),
            dma((SIDE,)),
        ],
        compiler_params=pltpu.CompilerParams(
            collective_id=0, has_side_effects=True, vmem_limit_bytes=63 * 1024 * 1024
        ),
    )(
        slot_clips,
        row_offsets,
        features.reshape(16, 32, 256),
        vae_weight.reshape(27, 256, 256),
        vae_gain.reshape(1, 256),
        vae_shift.reshape(1, 256),
        vae_bias.reshape(1, 256),
        latent_weight.T,
        latent_bias.reshape(1, 16),
        in_weight.reshape(9, 16, 320),
        in_bias,
        pos_table.T,
        unet_gain,
        unet_shift,
        unet_bias,
        unet_weight.reshape(9, 320, 320),
    )
    result = pl.pallas_call(
        hand_over,
        out_shape=jax.ShapeDtypeStruct((16, 16, 2, 1280), BF),
        in_specs=[hbm],
        out_specs=hbm,
        scratch_shapes=[pltpu.VMEM((16, 16, 2, 1280), BF), dma((2, 4))],
    )(result)
    return result.reshape(1, 16, 1, 16, 2, 1280)


def solution(mesh):
    return jax.shard_map(
        per_device,
        mesh=mesh,
        in_specs=(
            P("section", None, "slab", None, None, None),
            P(),
            P(),
            P(),
            P(),
            P(),
            P(),
            P(),
            P(),
            P(),
            P(),
            P(),
            P("section", None),
            P("section", None),
            P("section", None, None, None, None),
            P("section", None),
        ),
        out_specs=P("section", None, "slab", None, None, None),
        check_vma=False,
    )
```

```python
import jax
import jax.numpy as jnp
from jax import lax
from jax.experimental import pallas as pl
from jax.experimental.pallas import tpu as pltpu
from jax.sharding import PartitionSpec as P

BF = jnp.bfloat16
F32 = jnp.float32
MESH = pl.DeviceIdType.MESH
EPS = 1e-6
SIDE = 4
QUARTER = 240
CHUNKS = ((0, 64), (64, 64), (128, 64), (192, 48))


def group_matrix(used, width, group):
    a = lax.broadcasted_iota(jnp.int32, (width, width), 0)
    b = lax.broadcasted_iota(jnp.int32, (width, width), 1)
    same = (b - b % group) == (a - a % group)
    hit = jnp.logical_and(same, jnp.logical_and(a < used, b < used))
    return jnp.where(hit, 1.0, 0.0).astype(BF)


def partial_sums(values):
    return jnp.sum(values, axis=0), jnp.sum(values * values, axis=0)


def group_stats(partial, members, count):
    parts = []
    for eighths in partial:
        total = jnp.sum(eighths, axis=0, keepdims=True)
        high = total.astype(BF).astype(F32)
        rest = total - high
        mid = rest.astype(BF).astype(F32)
        parts += [high, mid, rest - mid]
    left = jnp.zeros_like(partial[0])
    row = lax.broadcasted_iota(jnp.int32, left.shape, 0)
    for index, part in enumerate(parts):
        left = jnp.where(row == index, part, left)
    sums = jnp.dot(left.astype(BF), members, preferred_element_type=F32)
    mean = (sums[0:1] + sums[1:2] + sums[2:3]) * (1.0 / count)
    meansq = (sums[3:4] + sums[4:5] + sums[5:6]) * (1.0 / count)
    return mean, lax.rsqrt(meansq - mean * mean + EPS)


def silu(v):
    half = 0.5 * v
    return half + half * jnp.tanh(half)


def across(left, right):
    return lax.dot_general(left, right, (((1,), (1,)), ((), ())), preferred_element_type=F32)


def up_down(values):
    zero = jnp.zeros_like(values[:1])
    return (
        jnp.concatenate([zero, values[:-1]], axis=0),
        jnp.concatenate([values[1:], zero], axis=0),
    )


def beside(values, step, cols):
    col = lax.broadcasted_iota(jnp.int32, values.shape, 1) % cols
    edge = 0 if step == 1 else cols - 1
    return jnp.where(col == edge, 0.0, pltpu.roll(values, step % 8, 1))


def block(y, stats, gain, shift, bias, weight):
    mean, inverse = stats
    act = silu((y - mean) * (inverse * gain) + shift)
    above, below = (a.reshape(128, 384) for a in up_down(act))
    here = act.reshape(128, 384)
    low = lax.broadcasted_iota(jnp.int32, (128, 128), 1) < 64
    tail = jnp.where(low, above[:, 256:], pltpu.roll(here[:, 256:], 64, 1))
    pieces = (above[:, :256], here[:, :256], below[:, :256], tail, below[:, 256:])
    left = jnp.concatenate([a.astype(BF) for a in pieces], axis=1)

    def product(n):
        return jnp.dot(left, weight[:, n * 256 : (n + 1) * 256], preferred_element_type=F32)

    def summed(before, middle, after, first, last):
        before, middle, after = (a.reshape(16, 8, last - first) for a in (before, middle, after))
        shifted = beside(before, 1, 4) + beside(after, -1, 4)
        return (y[:, :, first:last] + middle + shifted + bias[:, first:last]).astype(BF)

    tails = product(3)
    ends = tails[:, :128]
    high = summed(
        jnp.where(low, pltpu.roll(ends, 64, 1), 0.0),
        jnp.where(low, ends, 0.0),
        tails[:, 128:],
        256,
        384,
    )
    main = summed(product(0), product(1), product(2), 0, 256)
    return jnp.concatenate([main, high], axis=2)


def lay_out(y, spread):
    for n in range(3):
        spread[n] = y[:, :, n * 128 : (n + 1) * 128].reshape(128, 128)
    cells = []
    for col in range(4):
        every = pl.ds(col, 32, stride=4)
        cells += [spread[0, every, :], spread[1, every, :], spread[2, every, :][:, :64]]
    return jnp.concatenate(cells, axis=1).astype(BF).reshape(16, 2, 1280)


def fold(y, target):
    ends = y[:, 256:320]
    target[0:128, :] = y[:, :128].astype(BF)
    target[128:256, :] = y[:, 128:256].astype(BF)
    target[256:320, :] = jnp.concatenate([ends[:64], ends[64:]], axis=1).astype(BF)


def unfold(source):
    ends = source[256:320, :].astype(F32)
    low = lax.broadcasted_iota(jnp.int32, (64, 128), 1) < 64
    tops = jnp.where(low, ends, 0.0)
    bottoms = jnp.where(low, pltpu.roll(ends, 64, 1), 0.0)
    parts = (
        source[0:128, :].astype(F32),
        source[128:256, :].astype(F32),
        jnp.concatenate([tops, bottoms], axis=0),
    )
    return jnp.concatenate(parts, axis=1).reshape(16, 8, 384)


def pack_weight(raw, packed):
    packed[960:1024, :] = jnp.zeros((64, 1024), BF)
    for tap in range(3):
        for first, count, start in ((0, 256, tap * 256), (256, 64, 768 + 64 * tap)):
            rows = slice(start, start + count)
            ends = []
            for e in range(3):
                source = raw.at[tap * 3 + e]
                packed[rows, e * 256 : (e + 1) * 256] = source[first : first + count, :256]
                ends.append(source[first : first + count, 256:])
            packed[rows, 768:896] = jnp.concatenate([ends[1], ends[0]], axis=1)
            packed[rows, 896:1024] = jnp.concatenate([ends[2], jnp.zeros_like(ends[2])], axis=1)


def encode(clip, gain, shift, bias, weight, latent_weight, latent_bias):
    members = group_matrix(256, 256, 8)
    values = clip.astype(F32).reshape(64, 8, 256)
    mean, inverse = group_stats(partial_sums(values), members, 4096)
    act = silu((values - mean) * (inverse * gain) + shift).reshape(32, 2, 8, 256)
    lefts = []
    for frame in range(2):
        here = act[:, frame]
        above, below = up_down(here)
        lefts.append(
            jnp.concatenate([a.reshape(256, 256).astype(BF) for a in (above, here, below)], axis=1)
        )
    both = jnp.concatenate(lefts, axis=0)
    sums = [jnp.zeros((32, 8, 256), F32)] * 2
    for e in range(3):
        shared = jnp.dot(
            lefts[0], weight[e, 0:768, :], preferred_element_type=F32
        ) + jnp.dot(lefts[0], weight[e, 768:1536, :], preferred_element_type=F32)
        own = jnp.dot(both, weight[e, 1536:2304, :], preferred_element_type=F32)
        for frame in range(2):
            part = (shared + own[frame * 256 : (frame + 1) * 256]).reshape(32, 8, 256)
            sums[frame] = sums[frame] + (part if e == 1 else beside(part, 1 - e, 8))
    values = values.reshape(32, 2, 8, 256)
    paired = []
    for frame in range(2):
        summed = (values[:, frame] + sums[frame] + bias).reshape(16, 2, 8, 256)
        paired.append(summed[:, 0] + summed[:, 1])
    stacked = jnp.stack(paired, axis=1).reshape(256, 256)
    terms = []
    for _ in range(3):
        high = stacked.astype(BF)
        terms.append(high)
        stacked = stacked - high.astype(F32)
    row = lax.broadcasted_iota(jnp.int32, (128, 256), 0)
    col = lax.broadcasted_iota(jnp.int32, (128, 256), 1)
    pick = jnp.where(col - col % 2 == 2 * row, 1.0, 0.0).astype(BF)
    total = jnp.zeros((128, 256), F32)
    for high in terms:
        total = total + jnp.dot(pick, high, preferred_element_type=F32)
    pooled = (0.25 * total).astype(BF)
    latent = across(pooled, latent_weight) + latent_bias
    return latent.astype(BF).astype(F32)


def embed(latent, offset, weight, bias, table):
    grid = latent.reshape(16, 8, 16)
    columns = (beside(grid, 1, 4), grid, beside(grid, -1, 4))
    total = jnp.zeros((128, 320), F32)
    for e in range(3):
        above, below = up_down(columns[e])
        for b, rows in enumerate((above, columns[e], below)):
            total = total + jnp.dot(
                rows.reshape(128, 16).astype(BF), weight[b * 3 + e], preferred_element_type=F32
            )
    row = lax.broadcasted_iota(jnp.int32, (16, 8, 128), 0)
    entry = lax.broadcasted_iota(jnp.int32, (16, 8, 128), 2)
    one_hot = jnp.where(entry == row + offset, 1.0, 0.0).reshape(128, 128).astype(BF)
    placed = across(one_hot, table)
    return total + bias + placed


def kernel(
    slots_in,
    offsets_in,
    features_in,
    vae_weight,
    vae_gain_in,
    vae_shift_in,
    vae_bias_in,
    latent_weight_in,
    latent_bias_in,
    in_weight_in,
    in_bias_in,
    table_in,
    gain_in,
    shift_in,
    bias_in,
    unet_weight,
    out,
    slots,
    offsets,
    features,
    vae_gain,
    vae_shift,
    vae_bias,
    latent_weight,
    latent_bias,
    in_weight,
    in_bias,
    table,
    gain,
    shift,
    bias,
    staged,
    clip,
    encoder,
    raw,
    packed,
    norms,
    first_state,
    arriving,
    leaving,
    results,
    kept,
    spread,
    members,
    load_sem,
    small_sem,
    clip_send,
    clip_recv,
    norm_send,
    norm_recv,
    ring_send,
    ring_recv,
    pair_send,
    pair_recv,
    twin_send,
    twin_recv,
    first_send,
    state_send,
    state_recv,
    out_send,
    out_recv,
    keep_sem,
):
    section = lax.axis_index("section")
    slab = lax.axis_index("slab")
    x, y = section % SIDE, section // SIDE
    core = slab % 2
    parity = (slab // 2) % 2
    twin = slab + 1 - 2 * core

    def at_x(step):
        return {"section": y * SIDE + (x + step + SIDE) % SIDE}

    def remote(source, target, send, recv, device):
        return pltpu.make_async_remote_copy(
            src_ref=source,
            dst_ref=target,
            send_sem=send,
            recv_sem=recv,
            device_id=device,
            device_id_type=MESH,
        )

    weight_load = pltpu.make_async_copy(unet_weight, raw, load_sem.at[27])
    small = [
        pltpu.make_async_copy(source, target, small_sem.at[index])
        for index, (source, target) in enumerate(
            (
                (slots_in, slots),
                (offsets_in, offsets),
                (features_in, features),
                (gain_in, gain),
                (shift_in, shift),
                (bias_in, bias),
                (vae_gain_in, vae_gain),
                (vae_shift_in, vae_shift),
                (vae_bias_in, vae_bias),
                (latent_weight_in, latent_weight),
                (latent_bias_in, latent_bias),
                (in_weight_in, in_weight),
                (in_bias_in, in_bias),
                (table_in, table),
            )
        )
    ]

    def encoder_load(tap):
        a, b, e = tap // 9, (tap // 3) % 3, tap % 3
        return pltpu.make_async_copy(
            vae_weight.at[tap],
            encoder.at[e, pl.ds(a * 768 + b * 256, 256), :],
            load_sem.at[tap],
        )

    barrier = pltpu.get_barrier_semaphore()

    def greet(device):
        pl.semaphore_signal(barrier, 1, device_id=device, device_id_type=MESH)

    weight_load.start()

    @pl.loop(1, SIDE)
    def _(step):
        greet(at_x(step))
        greet({"section": ((y + step) % SIDE) * SIDE + x})

    @pl.loop(1, 16)
    def _(step):
        greet({"slab": (slab + step) % 16})

    for copy in small:
        copy.start()

    @pl.loop(0, 27)
    def _(tap):
        encoder_load(tap).start()

    for layer in range(SIDE):
        packed[layer, 960:1024, :] = jnp.zeros((64, 1024), BF)
    weight_load.wait()
    pack_weight(raw, packed.at[x])
    pl.semaphore_wait(barrier, 21)

    def chunk(owner, side, which, index):
        first, count = CHUNKS[index]
        start = (side * 2 + which) * QUARTER + first
        return packed.at[owner, pl.ds(pl.multiple_of(start, 16), count), :]

    def ring_copy(distance, index, from_left):
        step = 1 if from_left else -1
        owner = (x + step - distance + 2 * SIDE) % SIDE
        mine = chunk(owner, parity, core, index)
        at = (distance - 1) * 4 + index
        return remote(mine, mine, ring_send.at[at], ring_recv.at[at], at_x(step))

    def moved(distance, index, side, which, sems, device):
        owner = (x - distance + SIDE) % SIDE
        mine = chunk(owner, side, which, index)
        at = (distance - 1) * 4 + index
        return remote(mine, mine, sems[0].at[at], sems[1].at[at], device)

    ring = (ring_send, ring_recv)
    pair = (pair_send, pair_recv)
    twins = [(twin_send.at[n], twin_recv.at[n]) for n in range(2)]

    def along_z(index):
        return {"slab": (slab + (2 if index < 2 else 14)) % 16}

    events = [(1, 0), (3, 2), (1, 1), (3, 3), (2, 0), (2, 2), (2, 1), (2, 3), (1, 2), (3, 0), (1, 3), (3, 1)]
    relays = {(1, 0): True, (1, 1): True, (3, 2): False, (3, 3): False}
    own_sends = [(1, 0, True), (3, 2, False), (1, 1, True), (3, 3, False)]
    own_sends += [(1, 2, True), (3, 0, False), (1, 3, True), (3, 1, False)]
    ring_sends = own_sends + [(2, event[1], way) for event, way in relays.items()]

    def on_ring(number):
        distance, index = events[number]
        moved(distance, index, parity, core, ring, at_x(1)).wait_recv()
        if events[number] in relays:
            ring_copy(2, index, relays[events[number]]).start()
        moved(distance, index, parity, core, pair, along_z(index)).start()
        moved(distance, index, parity, core, twins[0], {"slab": twin}).start()

    def on_pair(number):
        distance, index = events[number]
        moved(distance, index, 1 - parity, core, pair, along_z(index)).wait_recv()
        moved(distance, index, 1 - parity, core, twins[1], {"slab": twin}).start()

    for distance, index, from_left in own_sends[:4]:
        ring_copy(distance, index, from_left).start()

    for copy in small:
        copy.wait()

    @pl.loop(0, 16)
    def _(slot):
        staged[slot] = features[slots[section, slot]]


    def clip_copy(step):
        to = (slab + step) % 16
        return remote(
            staged.at[to], clip.at[slab], clip_send.at[step], clip_recv.at[step], {"slab": to}
        )

    def clip_arrival(step):
        return remote(
            staged.at[slab],
            clip.at[(slab + 16 - step) % 16],
            clip_send.at[step],
            clip_recv.at[step],
            {"slab": (slab + step) % 16},
        )

    @pl.loop(1, 16)
    def _(step):
        clip_copy(step).start()

    norms[x] = jnp.zeros((8, 384), F32)
    norms[x, 0:1, 0:320] = gain[...]
    norms[x, 1:2, 0:320] = shift[...]
    norms[x, 2:3, 0:320] = bias[...]

    def norm_copy(step, owner):
        return remote(
            norms.at[owner], norms.at[owner], norm_send.at[step], norm_recv.at[step], at_x(step)
        )

    @pl.loop(1, SIDE)
    def _(step):
        norm_copy(step, x).start()

    clip[slab] = staged[slab]
    members[...] = group_matrix(320, 384, 10)

    @pl.loop(0, 27)
    def _(tap):
        encoder_load(tap).wait()

    for number in range(4):
        on_ring(number)
    for distance, index, from_left in own_sends[4:]:
        ring_copy(distance, index, from_left).start()

    for number in range(4, 12):
        on_ring(number)
        on_pair(number - 4)

    @pl.loop(1, 16)
    def _(step):
        clip_arrival(step).wait_recv()

    latent = encode(
        clip[...].reshape(512, 256),
        vae_gain[...],
        vae_shift[...],
        vae_bias[...],
        encoder,
        latent_weight[...],
        latent_bias[...],
    )
    offset = offsets[section, slots[section, slab]]
    embedded = embed(latent, offset, in_weight, in_bias[...].reshape(1, 320), table[...])
    fold(embedded, first_state)

    def first_copy():
        return remote(
            first_state, arriving.at[y], first_send, state_recv.at[y], {"section": x}
        )

    @pl.when(y == 0)
    def _():
        arriving[0] = first_state[...]

    @pl.when(y > 0)
    def _():
        first_copy().start()

    for number in range(8, 12):
        on_pair(number)

    @pl.loop(1, SIDE)
    def _(step):
        norm_copy(step, (x + SIDE - step) % SIDE).wait_recv()

    for distance, index in events:
        for n in range(2):
            side = parity if n == 0 else 1 - parity
            moved(distance, index, side, 1 - core, twins[n], {"slab": twin}).wait_recv()

    def state_copy(turn):
        return remote(
            leaving.at[turn],
            arriving.at[turn],
            state_send.at[turn],
            state_recv.at[turn],
            {"section": (section + SIDE) % 16},
        )

    def out_copy(index):
        turn, layer = index // SIDE, index % SIDE
        micro = turn * SIDE + x
        return remote(
            results.at[index],
            out.at[micro],
            out_send.at[index],
            out_recv.at[micro],
            {"section": y * SIDE + layer},
        )

    def out_arrival(micro):
        return remote(
            results.at[micro],
            out.at[micro],
            out_send.at[micro],
            out_recv.at[micro],
            {"section": y * SIDE + micro % SIDE},
        )

    def keep_copy(turn):
        index = turn * SIDE + x
        return pltpu.make_async_copy(results.at[index], out.at[index], keep_sem.at[turn])

    def push(turn, layer):
        @pl.when(layer == x)
        def _():
            keep_copy(turn).start()

        @pl.when(layer != x)
        def _():
            out_copy(turn * SIDE + layer).start()

    @pl.loop(0, SIDE)
    def _(turn):
        @pl.when(turn + y > 0)
        def _():
            state_copy(turn).wait_recv()

        state = unfold(arriving.at[turn])
        partial = partial_sums(state)
        for layer in range(SIDE):
            stats = group_stats(partial, members[...], 1280)
            if layer > 0:
                results[turn * SIDE + layer - 1] = lay_out(state, spread)
            result = block(
                state,
                stats,
                norms[layer, 0:1, :],
                norms[layer, 1:2, :],
                norms[layer, 2:3, :],
                packed.at[layer],
            )
            if layer == SIDE - 1:

                @pl.when(y < SIDE - 1)
                def _():
                    fold(result.astype(F32).reshape(128, 384), leaving.at[turn])
                    state_copy(turn).start()

            state = result.astype(F32)
            partial = partial_sums(state)
            kept[...] = state
            state = kept[...]
            if layer > 0:
                push(turn, layer - 1)
        results[turn * SIDE + SIDE - 1] = lay_out(state, spread)
        push(turn, SIDE - 1)

    @pl.when(y > 0)
    def _():
        first_copy().wait_send()

    @pl.loop(1, 16)
    def _(step):
        clip_copy(step).wait_send()

    @pl.loop(1, SIDE)
    def _(step):
        norm_copy(step, x).wait_send()

    for distance, index, from_left in ring_sends:
        ring_copy(distance, index, from_left).wait_send()
    for distance, index in events:
        moved(distance, index, parity, core, pair, along_z(index)).wait_send()
        for n in range(2):
            side = parity if n == 0 else 1 - parity
            moved(distance, index, side, core, twins[n], {"slab": twin}).wait_send()

    @pl.loop(0, SIDE)
    def _(turn):
        keep_copy(turn).wait()

        @pl.when(y < SIDE - 1)
        def _():
            state_copy(turn).wait_send()

    @pl.loop(0, 16)
    def _(index):
        @pl.when(index % SIDE != x)
        def _():
            out_copy(index).wait_send()
            out_arrival(index).wait_recv()


def hand_over(source, target, buffer, sems):
    parts = [pl.ds(n * 4, 4) for n in range(4)]
    loads = [pltpu.make_async_copy(source.at[p], buffer.at[p], sems.at[0, n]) for n, p in enumerate(parts)]
    stores = [pltpu.make_async_copy(buffer.at[p], target.at[p], sems.at[1, n]) for n, p in enumerate(parts)]
    for copy in loads:
        copy.start()
    for load, store in zip(loads, stores):
        load.wait()
        store.start()
    for copy in stores:
        copy.wait()


def per_device(
    features,
    vae_weight,
    vae_gain,
    vae_shift,
    vae_bias,
    latent_weight,
    latent_bias,
    slot_clips,
    row_offsets,
    in_weight,
    in_bias,
    pos_table,
    unet_gain,
    unet_shift,
    unet_weight,
    unet_bias,
):
    hbm = pl.BlockSpec(memory_space=pltpu.HBM)
    anywhere = pl.BlockSpec(memory_space=pl.ANY)
    dma = pltpu.SemaphoreType.DMA
    result = pl.pallas_call(
        kernel,
        out_shape=jax.ShapeDtypeStruct((16, 16, 2, 1280), BF),
        in_specs=[hbm] * 16,
        out_specs=anywhere,
        scratch_shapes=[
            pltpu.SMEM((16, 16), jnp.int32),
            pltpu.SMEM((16, 16), jnp.int32),
            pltpu.VMEM((16, 32, 256), BF),
            pltpu.VMEM((1, 256), F32),
            pltpu.VMEM((1, 256), F32),
            pltpu.VMEM((1, 256), F32),
            pltpu.VMEM((16, 256), BF),
            pltpu.VMEM((1, 16), F32),
            pltpu.VMEM((9, 16, 320), BF),
            pltpu.VMEM((320,), F32),
            pltpu.VMEM((320, 128), BF),
            pltpu.VMEM((1, 320), F32),
            pltpu.VMEM((1, 320), F32),
            pltpu.VMEM((1, 320), F32),
            pltpu.VMEM((16, 32, 256), BF),
            pltpu.VMEM((16, 32, 256), BF),
            pltpu.VMEM((3, 2304, 256), BF),
            pltpu.VMEM((9, 320, 320), BF),
            pltpu.VMEM((SIDE, 1024, 1024), BF),
            pltpu.VMEM((SIDE, 8, 384), F32),
            pltpu.VMEM((320, 128), BF),
            pltpu.VMEM((SIDE, 320, 128), BF),
            pltpu.VMEM((SIDE, 320, 128), BF),
            pltpu.VMEM((16, 16, 2, 1280), BF),
            pltpu.VMEM((16, 8, 384), F32),
            pltpu.VMEM((3, 128, 128), F32),
            pltpu.VMEM((384, 384), BF),
            dma((28,)),
            dma((14,)),
            dma((16,)),
            dma((16,)),
            dma((SIDE,)),
            dma((SIDE,)),
            dma((12,)),
            dma((12,)),
            dma((12,)),
            dma((12,)),
            dma((2, 12)),
            dma((2, 12)),
            dma,
            dma((SIDE,)),
            dma((SIDE,)),
            dma((16,)),
            dma((16,)),
            dma((SIDE,)),
        ],
        compiler_params=pltpu.CompilerParams(
            collective_id=0, has_side_effects=True, vmem_limit_bytes=63 * 1024 * 1024
        ),
    )(
        slot_clips,
        row_offsets,
        features.reshape(16, 32, 256),
        vae_weight.reshape(27, 256, 256),
        vae_gain.reshape(1, 256),
        vae_shift.reshape(1, 256),
        vae_bias.reshape(1, 256),
        latent_weight.T,
        latent_bias.reshape(1, 16),
        in_weight.reshape(9, 16, 320),
        in_bias,
        pos_table.T,
        unet_gain,
        unet_shift,
        unet_bias,
        unet_weight.reshape(9, 320, 320),
    )
    result = pl.pallas_call(
        hand_over,
        out_shape=jax.ShapeDtypeStruct((16, 16, 2, 1280), BF),
        in_specs=[hbm],
        out_specs=hbm,
        scratch_shapes=[pltpu.VMEM((16, 16, 2, 1280), BF), dma((2, 4))],
    )(result)
    return result.reshape(1, 16, 1, 16, 2, 1280)


def solution(mesh):
    return jax.shard_map(
        per_device,
        mesh=mesh,
        in_specs=(
            P("section", None, "slab", None, None, None),
            P(),
            P(),
            P(),
            P(),
            P(),
            P(),
            P(),
            P(),
            P(),
            P(),
            P(),
            P("section", None),
            P("section", None),
            P("section", None, None, None, None),
            P("section", None),
        ),
        out_specs=P("section", None, "slab", None, None, None),
        check_vma=False,
    )
```

```python
import jax
import jax.numpy as jnp
from jax import lax
from jax.experimental import pallas as pl
from jax.experimental.pallas import tpu as pltpu
from jax.sharding import PartitionSpec as P

BF = jnp.bfloat16
F32 = jnp.float32
MESH = pl.DeviceIdType.MESH
EPS = 1e-6
SIDE = 4
QUARTER = 240
CHUNKS = ((0, 64), (64, 48), (112, 16), (128, 64), (192, 32), (224, 16))
FIRST = 3


def group_matrix(used, width, group):
    a = lax.broadcasted_iota(jnp.int32, (width, width), 0)
    b = lax.broadcasted_iota(jnp.int32, (width, width), 1)
    same = (b - b % group) == (a - a % group)
    hit = jnp.logical_and(same, jnp.logical_and(a < used, b < used))
    return jnp.where(hit, 1.0, 0.0).astype(BF)


def partial_sums(values):
    return jnp.sum(values, axis=0), jnp.sum(values * values, axis=0)


def group_stats(partial, members, count):
    parts = []
    for eighths in partial:
        total = jnp.sum(eighths, axis=0, keepdims=True)
        high = total.astype(BF).astype(F32)
        rest = total - high
        mid = rest.astype(BF).astype(F32)
        parts += [high, mid, rest - mid]
    left = jnp.zeros_like(partial[0])
    row = lax.broadcasted_iota(jnp.int32, left.shape, 0)
    for index, part in enumerate(parts):
        left = jnp.where(row == index, part, left)
    sums = jnp.dot(left.astype(BF), members, preferred_element_type=F32)
    mean = (sums[0:1] + sums[1:2] + sums[2:3]) * (1.0 / count)
    meansq = (sums[3:4] + sums[4:5] + sums[5:6]) * (1.0 / count)
    return mean, lax.rsqrt(meansq - mean * mean + EPS)


def silu(v):
    half = 0.5 * v
    return half + half * jnp.tanh(half)


def across(left, right):
    return lax.dot_general(left, right, (((1,), (1,)), ((), ())), preferred_element_type=F32)


def up_down(values):
    zero = jnp.zeros_like(values[:1])
    return (
        jnp.concatenate([zero, values[:-1]], axis=0),
        jnp.concatenate([values[1:], zero], axis=0),
    )


def beside(values, step, cols):
    col = lax.broadcasted_iota(jnp.int32, values.shape, 1) % cols
    edge = 0 if step == 1 else cols - 1
    return jnp.where(col == edge, 0.0, pltpu.roll(values, step % 8, 1))


def block(y, stats, gain, shift, bias, weight):
    mean, inverse = stats
    act = silu((y - mean) * (inverse * gain) + shift)
    above, below = (a.reshape(128, 384) for a in up_down(act))
    here = act.reshape(128, 384)
    low = lax.broadcasted_iota(jnp.int32, (128, 128), 1) < 64
    tail = jnp.where(low, above[:, 256:], pltpu.roll(here[:, 256:], 64, 1))
    pieces = (above[:, :256], here[:, :256], below[:, :256], tail, below[:, 256:])
    left = jnp.concatenate([a.astype(BF) for a in pieces], axis=1)

    def product(n):
        return jnp.dot(left, weight[:, n * 256 : (n + 1) * 256], preferred_element_type=F32)

    def summed(before, middle, after, first, last):
        before, middle, after = (a.reshape(16, 8, last - first) for a in (before, middle, after))
        shifted = beside(before, 1, 4) + beside(after, -1, 4)
        return (y[:, :, first:last] + middle + shifted + bias[:, first:last]).astype(BF)

    tails = product(3)
    ends = tails[:, :128]
    high = summed(
        jnp.where(low, pltpu.roll(ends, 64, 1), 0.0),
        jnp.where(low, ends, 0.0),
        tails[:, 128:],
        256,
        384,
    )
    main = summed(product(0), product(1), product(2), 0, 256)
    return jnp.concatenate([main, high], axis=2)


def lay_out(y, spread):
    for n in range(3):
        spread[n] = y[:, :, n * 128 : (n + 1) * 128].reshape(128, 128)
    cells = []
    for col in range(4):
        every = pl.ds(col, 32, stride=4)
        cells += [spread[0, every, :], spread[1, every, :], spread[2, every, :][:, :64]]
    return jnp.concatenate(cells, axis=1).astype(BF).reshape(16, 2, 1280)


def fold(y, target):
    ends = y[:, 256:320]
    target[0:128, :] = y[:, :128].astype(BF)
    target[128:256, :] = y[:, 128:256].astype(BF)
    target[256:320, :] = jnp.concatenate([ends[:64], ends[64:]], axis=1).astype(BF)


def unfold(source):
    ends = source[256:320, :].astype(F32)
    low = lax.broadcasted_iota(jnp.int32, (64, 128), 1) < 64
    tops = jnp.where(low, ends, 0.0)
    bottoms = jnp.where(low, pltpu.roll(ends, 64, 1), 0.0)
    parts = (
        source[0:128, :].astype(F32),
        source[128:256, :].astype(F32),
        jnp.concatenate([tops, bottoms], axis=0),
    )
    return jnp.concatenate(parts, axis=1).reshape(16, 8, 384)


def pack_weight(raw, packed):
    packed[960:1024, :] = jnp.zeros((64, 1024), BF)
    for tap in range(3):
        for first, count, start in ((0, 256, tap * 256), (256, 64, 768 + 64 * tap)):
            rows = slice(start, start + count)
            ends = []
            for e in range(3):
                source = raw.at[tap * 3 + e]
                packed[rows, e * 256 : (e + 1) * 256] = source[first : first + count, :256]
                ends.append(source[first : first + count, 256:])
            packed[rows, 768:896] = jnp.concatenate([ends[1], ends[0]], axis=1)
            packed[rows, 896:1024] = jnp.concatenate([ends[2], jnp.zeros_like(ends[2])], axis=1)


def encode(clip, gain, shift, bias, weight, latent_weight, latent_bias):
    members = group_matrix(256, 256, 8)
    values = clip.astype(F32).reshape(64, 8, 256)
    mean, inverse = group_stats(partial_sums(values), members, 4096)
    act = silu((values - mean) * (inverse * gain) + shift).reshape(32, 2, 8, 256)
    lefts = []
    for frame in range(2):
        here = act[:, frame]
        above, below = up_down(here)
        lefts.append(
            jnp.concatenate([a.reshape(256, 256).astype(BF) for a in (above, here, below)], axis=1)
        )
    both = jnp.concatenate(lefts, axis=0)
    sums = [jnp.zeros((32, 8, 256), F32)] * 2
    for e in range(3):
        shared = jnp.dot(
            lefts[0], weight[e, 0:768, :], preferred_element_type=F32
        ) + jnp.dot(lefts[0], weight[e, 768:1536, :], preferred_element_type=F32)
        own = jnp.dot(both, weight[e, 1536:2304, :], preferred_element_type=F32)
        for frame in range(2):
            part = (shared + own[frame * 256 : (frame + 1) * 256]).reshape(32, 8, 256)
            sums[frame] = sums[frame] + (part if e == 1 else beside(part, 1 - e, 8))
    values = values.reshape(32, 2, 8, 256)
    paired = []
    for frame in range(2):
        summed = (values[:, frame] + sums[frame] + bias).reshape(16, 2, 8, 256)
        paired.append(summed[:, 0] + summed[:, 1])
    stacked = jnp.stack(paired, axis=1).reshape(256, 256)
    terms = []
    for _ in range(3):
        high = stacked.astype(BF)
        terms.append(high)
        stacked = stacked - high.astype(F32)
    row = lax.broadcasted_iota(jnp.int32, (128, 256), 0)
    col = lax.broadcasted_iota(jnp.int32, (128, 256), 1)
    pick = jnp.where(col - col % 2 == 2 * row, 1.0, 0.0).astype(BF)
    total = jnp.zeros((128, 256), F32)
    for high in terms:
        total = total + jnp.dot(pick, high, preferred_element_type=F32)
    pooled = (0.25 * total).astype(BF)
    latent = across(pooled, latent_weight) + latent_bias
    return latent.astype(BF).astype(F32)


def embed(latent, offset, weight, bias, table):
    grid = latent.reshape(16, 8, 16)
    columns = (beside(grid, 1, 4), grid, beside(grid, -1, 4))
    total = jnp.zeros((128, 320), F32)
    for e in range(3):
        above, below = up_down(columns[e])
        for b, rows in enumerate((above, columns[e], below)):
            total = total + jnp.dot(
                rows.reshape(128, 16).astype(BF), weight[b * 3 + e], preferred_element_type=F32
            )
    row = lax.broadcasted_iota(jnp.int32, (16, 8, 128), 0)
    entry = lax.broadcasted_iota(jnp.int32, (16, 8, 128), 2)
    one_hot = jnp.where(entry == row + offset, 1.0, 0.0).reshape(128, 128).astype(BF)
    placed = across(one_hot, table)
    return total + bias + placed


def kernel(
    slots_in,
    offsets_in,
    features_in,
    vae_weight,
    vae_gain_in,
    vae_shift_in,
    vae_bias_in,
    latent_weight_in,
    latent_bias_in,
    in_weight_in,
    in_bias_in,
    table_in,
    gain_in,
    shift_in,
    bias_in,
    unet_weight,
    out,
    slots,
    offsets,
    features,
    vae_gain,
    vae_shift,
    vae_bias,
    latent_weight,
    latent_bias,
    in_weight,
    in_bias,
    table,
    gain,
    shift,
    bias,
    staged,
    clip,
    encoder,
    raw,
    packed,
    norms,
    first_state,
    arriving,
    leaving,
    results,
    kept,
    spread,
    members,
    load_sem,
    small_sem,
    clip_send,
    clip_recv,
    norm_send,
    norm_recv,
    ring_send,
    ring_recv,
    pair_send,
    pair_recv,
    twin_send,
    twin_recv,
    first_send,
    state_send,
    state_recv,
    out_send,
    out_recv,
    keep_sem,
):
    section = lax.axis_index("section")
    slab = lax.axis_index("slab")
    x, y = section % SIDE, section // SIDE
    core = slab % 2
    parity = (slab // 2) % 2
    twin = slab + 1 - 2 * core

    def at_x(step):
        return {"section": y * SIDE + (x + step + SIDE) % SIDE}

    def remote(source, target, send, recv, device):
        return pltpu.make_async_remote_copy(
            src_ref=source,
            dst_ref=target,
            send_sem=send,
            recv_sem=recv,
            device_id=device,
            device_id_type=MESH,
        )

    weight_load = pltpu.make_async_copy(unet_weight, raw, load_sem.at[27])
    small = [
        pltpu.make_async_copy(source, target, small_sem.at[index])
        for index, (source, target) in enumerate(
            (
                (slots_in, slots),
                (offsets_in, offsets),
                (features_in, features),
                (gain_in, gain),
                (shift_in, shift),
                (bias_in, bias),
                (vae_gain_in, vae_gain),
                (vae_shift_in, vae_shift),
                (vae_bias_in, vae_bias),
                (latent_weight_in, latent_weight),
                (latent_bias_in, latent_bias),
                (in_weight_in, in_weight),
                (in_bias_in, in_bias),
                (table_in, table),
            )
        )
    ]

    def encoder_load(tap):
        a, b, e = tap // 9, (tap // 3) % 3, tap % 3
        return pltpu.make_async_copy(
            vae_weight.at[tap],
            encoder.at[e, pl.ds(a * 768 + b * 256, 256), :],
            load_sem.at[tap],
        )

    barrier = pltpu.get_barrier_semaphore()

    def greet(device):
        pl.semaphore_signal(barrier, 1, device_id=device, device_id_type=MESH)

    weight_load.start()

    @pl.loop(1, SIDE)
    def _(step):
        greet(at_x(step))
        greet({"section": ((y + step) % SIDE) * SIDE + x})

    @pl.loop(1, 16)
    def _(step):
        greet({"slab": (slab + step) % 16})

    for copy in small:
        copy.start()

    @pl.loop(0, 27)
    def _(tap):
        encoder_load(tap).start()

    for layer in range(SIDE):
        packed[layer, 960:1024, :] = jnp.zeros((64, 1024), BF)
    weight_load.wait()
    pack_weight(raw, packed.at[x])
    pl.semaphore_wait(barrier, 21)

    def chunk(owner, side, which, index):
        first, count = CHUNKS[index]
        start = (side * 2 + which) * QUARTER + first
        return packed.at[owner, pl.ds(pl.multiple_of(start, 16), count), :]

    def ring_copy(distance, index, from_left):
        step = 1 if from_left else -1
        owner = (x + step - distance + 2 * SIDE) % SIDE
        mine = chunk(owner, parity, core, index)
        at = (distance - 1) * len(CHUNKS) + index
        return remote(mine, mine, ring_send.at[at], ring_recv.at[at], at_x(step))

    def moved(distance, index, side, which, sems, device):
        owner = (x - distance + SIDE) % SIDE
        mine = chunk(owner, side, which, index)
        at = (distance - 1) * len(CHUNKS) + index
        return remote(mine, mine, sems[0].at[at], sems[1].at[at], device)

    ring = (ring_send, ring_recv)
    pair = (pair_send, pair_recv)
    twins = [(twin_send.at[n], twin_recv.at[n]) for n in range(2)]

    def along_z(index):
        return {"slab": (slab + (2 if index < FIRST else 14)) % 16}

    def in_turn(first, second):
        return [event for both in zip(first, second) for event in both]

    rightmost, leftmost = range(FIRST), range(FIRST, len(CHUNKS))
    relayed = in_turn([(1, n) for n in rightmost], [(3, n) for n in leftmost])
    opposite = in_turn([(2, n) for n in rightmost], [(2, n) for n in leftmost])
    others = in_turn([(1, n) for n in leftmost], [(3, n) for n in rightmost])
    events = relayed + opposite + others
    early = len(relayed)
    relays = {event: event[0] == 1 for event in relayed}
    own_sends = [(distance, index, distance == 1) for distance, index in relayed + others]
    ring_sends = own_sends + [(2, event[1], way) for event, way in relays.items()]

    def on_ring(number):
        distance, index = events[number]
        moved(distance, index, parity, core, ring, at_x(1)).wait_recv()
        if events[number] in relays:
            ring_copy(2, index, relays[events[number]]).start()
        moved(distance, index, parity, core, pair, along_z(index)).start()
        moved(distance, index, parity, core, twins[0], {"slab": twin}).start()

    def on_pair(number):
        distance, index = events[number]
        moved(distance, index, 1 - parity, core, pair, along_z(index)).wait_recv()
        moved(distance, index, 1 - parity, core, twins[1], {"slab": twin}).start()

    for distance, index, from_left in own_sends[:early]:
        ring_copy(distance, index, from_left).start()

    for copy in small:
        copy.wait()

    @pl.loop(0, 16)
    def _(slot):
        staged[slot] = features[slots[section, slot]]


    def clip_copy(step):
        to = (slab + step) % 16
        return remote(
            staged.at[to], clip.at[slab], clip_send.at[step], clip_recv.at[step], {"slab": to}
        )

    def clip_arrival(step):
        return remote(
            staged.at[slab],
            clip.at[(slab + 16 - step) % 16],
            clip_send.at[step],
            clip_recv.at[step],
            {"slab": (slab + step) % 16},
        )

    @pl.loop(1, 16)
    def _(step):
        clip_copy(step).start()

    norms[x] = jnp.zeros((8, 384), F32)
    norms[x, 0:1, 0:320] = gain[...]
    norms[x, 1:2, 0:320] = shift[...]
    norms[x, 2:3, 0:320] = bias[...]

    def norm_copy(step, owner):
        return remote(
            norms.at[owner], norms.at[owner], norm_send.at[step], norm_recv.at[step], at_x(step)
        )

    @pl.loop(1, SIDE)
    def _(step):
        norm_copy(step, x).start()

    clip[slab] = staged[slab]
    members[...] = group_matrix(320, 384, 10)

    @pl.loop(0, 27)
    def _(tap):
        encoder_load(tap).wait()

    for number in range(early):
        on_ring(number)
    for distance, index, from_left in own_sends[early:]:
        ring_copy(distance, index, from_left).start()

    for number in range(early, len(events)):
        on_ring(number)
        on_pair(number - early)

    @pl.loop(1, 16)
    def _(step):
        clip_arrival(step).wait_recv()

    latent = encode(
        clip[...].reshape(512, 256),
        vae_gain[...],
        vae_shift[...],
        vae_bias[...],
        encoder,
        latent_weight[...],
        latent_bias[...],
    )
    offset = offsets[section, slots[section, slab]]
    embedded = embed(latent, offset, in_weight, in_bias[...].reshape(1, 320), table[...])
    fold(embedded, first_state)

    def first_copy():
        return remote(
            first_state, arriving.at[y], first_send, state_recv.at[y], {"section": x}
        )

    @pl.when(y == 0)
    def _():
        arriving[0] = first_state[...]

    @pl.when(y > 0)
    def _():
        first_copy().start()

    for number in range(len(events) - early, len(events)):
        on_pair(number)

    @pl.loop(1, SIDE)
    def _(step):
        norm_copy(step, (x + SIDE - step) % SIDE).wait_recv()

    for distance, index in events:
        for n in range(2):
            side = parity if n == 0 else 1 - parity
            moved(distance, index, side, 1 - core, twins[n], {"slab": twin}).wait_recv()

    def state_copy(turn):
        return remote(
            leaving.at[turn],
            arriving.at[turn],
            state_send.at[turn],
            state_recv.at[turn],
            {"section": (section + SIDE) % 16},
        )

    def out_copy(index):
        turn, layer = index // SIDE, index % SIDE
        micro = turn * SIDE + x
        return remote(
            results.at[index],
            out.at[micro],
            out_send.at[index],
            out_recv.at[micro],
            {"section": y * SIDE + layer},
        )

    def out_arrival(micro):
        return remote(
            results.at[micro],
            out.at[micro],
            out_send.at[micro],
            out_recv.at[micro],
            {"section": y * SIDE + micro % SIDE},
        )

    def keep_copy(turn):
        index = turn * SIDE + x
        return pltpu.make_async_copy(results.at[index], out.at[index], keep_sem.at[turn])

    def push(turn, layer):
        @pl.when(layer == x)
        def _():
            keep_copy(turn).start()

        @pl.when(layer != x)
        def _():
            out_copy(turn * SIDE + layer).start()

    @pl.loop(0, SIDE)
    def _(turn):
        @pl.when(turn + y > 0)
        def _():
            state_copy(turn).wait_recv()

        state = unfold(arriving.at[turn])
        partial = partial_sums(state)
        for layer in range(SIDE):
            stats = group_stats(partial, members[...], 1280)
            if layer > 0:
                results[turn * SIDE + layer - 1] = lay_out(state, spread)
            result = block(
                state,
                stats,
                norms[layer, 0:1, :],
                norms[layer, 1:2, :],
                norms[layer, 2:3, :],
                packed.at[layer],
            )
            if layer == SIDE - 1:

                @pl.when(y < SIDE - 1)
                def _():
                    fold(result.astype(F32).reshape(128, 384), leaving.at[turn])
                    state_copy(turn).start()

            state = result.astype(F32)
            partial = partial_sums(state)
            kept[...] = state
            state = kept[...]
            if layer > 0:
                push(turn, layer - 1)
        results[turn * SIDE + SIDE - 1] = lay_out(state, spread)
        push(turn, SIDE - 1)

    @pl.when(y > 0)
    def _():
        first_copy().wait_send()

    @pl.loop(1, 16)
    def _(step):
        clip_copy(step).wait_send()

    @pl.loop(1, SIDE)
    def _(step):
        norm_copy(step, x).wait_send()

    for distance, index, from_left in ring_sends:
        ring_copy(distance, index, from_left).wait_send()
    for distance, index in events:
        moved(distance, index, parity, core, pair, along_z(index)).wait_send()
        for n in range(2):
            side = parity if n == 0 else 1 - parity
            moved(distance, index, side, core, twins[n], {"slab": twin}).wait_send()

    @pl.loop(0, SIDE)
    def _(turn):
        keep_copy(turn).wait()

        @pl.when(y < SIDE - 1)
        def _():
            state_copy(turn).wait_send()

    @pl.loop(0, 16)
    def _(index):
        @pl.when(index % SIDE != x)
        def _():
            out_copy(index).wait_send()
            out_arrival(index).wait_recv()


def hand_over(source, target, buffer, sems):
    parts = [pl.ds(n * 4, 4) for n in range(4)]
    loads = [pltpu.make_async_copy(source.at[p], buffer.at[p], sems.at[0, n]) for n, p in enumerate(parts)]
    stores = [pltpu.make_async_copy(buffer.at[p], target.at[p], sems.at[1, n]) for n, p in enumerate(parts)]
    for copy in loads:
        copy.start()
    for load, store in zip(loads, stores):
        load.wait()
        store.start()
    for copy in stores:
        copy.wait()


def per_device(
    features,
    vae_weight,
    vae_gain,
    vae_shift,
    vae_bias,
    latent_weight,
    latent_bias,
    slot_clips,
    row_offsets,
    in_weight,
    in_bias,
    pos_table,
    unet_gain,
    unet_shift,
    unet_weight,
    unet_bias,
):
    hbm = pl.BlockSpec(memory_space=pltpu.HBM)
    anywhere = pl.BlockSpec(memory_space=pl.ANY)
    dma = pltpu.SemaphoreType.DMA
    result = pl.pallas_call(
        kernel,
        out_shape=jax.ShapeDtypeStruct((16, 16, 2, 1280), BF),
        in_specs=[hbm] * 16,
        out_specs=anywhere,
        scratch_shapes=[
            pltpu.SMEM((16, 16), jnp.int32),
            pltpu.SMEM((16, 16), jnp.int32),
            pltpu.VMEM((16, 32, 256), BF),
            pltpu.VMEM((1, 256), F32),
            pltpu.VMEM((1, 256), F32),
            pltpu.VMEM((1, 256), F32),
            pltpu.VMEM((16, 256), BF),
            pltpu.VMEM((1, 16), F32),
            pltpu.VMEM((9, 16, 320), BF),
            pltpu.VMEM((320,), F32),
            pltpu.VMEM((320, 128), BF),
            pltpu.VMEM((1, 320), F32),
            pltpu.VMEM((1, 320), F32),
            pltpu.VMEM((1, 320), F32),
            pltpu.VMEM((16, 32, 256), BF),
            pltpu.VMEM((16, 32, 256), BF),
            pltpu.VMEM((3, 2304, 256), BF),
            pltpu.VMEM((9, 320, 320), BF),
            pltpu.VMEM((SIDE, 1024, 1024), BF),
            pltpu.VMEM((SIDE, 8, 384), F32),
            pltpu.VMEM((320, 128), BF),
            pltpu.VMEM((SIDE, 320, 128), BF),
            pltpu.VMEM((SIDE, 320, 128), BF),
            pltpu.VMEM((16, 16, 2, 1280), BF),
            pltpu.VMEM((16, 8, 384), F32),
            pltpu.VMEM((3, 128, 128), F32),
            pltpu.VMEM((384, 384), BF),
            dma((28,)),
            dma((14,)),
            dma((16,)),
            dma((16,)),
            dma((SIDE,)),
            dma((SIDE,)),
            dma((18,)),
            dma((18,)),
            dma((18,)),
            dma((18,)),
            dma((2, 18)),
            dma((2, 18)),
            dma,
            dma((SIDE,)),
            dma((SIDE,)),
            dma((16,)),
            dma((16,)),
            dma((SIDE,)),
        ],
        compiler_params=pltpu.CompilerParams(
            collective_id=0, has_side_effects=True, vmem_limit_bytes=63 * 1024 * 1024
        ),
    )(
        slot_clips,
        row_offsets,
        features.reshape(16, 32, 256),
        vae_weight.reshape(27, 256, 256),
        vae_gain.reshape(1, 256),
        vae_shift.reshape(1, 256),
        vae_bias.reshape(1, 256),
        latent_weight.T,
        latent_bias.reshape(1, 16),
        in_weight.reshape(9, 16, 320),
        in_bias,
        pos_table.T,
        unet_gain,
        unet_shift,
        unet_bias,
        unet_weight.reshape(9, 320, 320),
    )
    result = pl.pallas_call(
        hand_over,
        out_shape=jax.ShapeDtypeStruct((16, 16, 2, 1280), BF),
        in_specs=[hbm],
        out_specs=hbm,
        scratch_shapes=[pltpu.VMEM((16, 16, 2, 1280), BF), dma((2, 4))],
    )(result)
    return result.reshape(1, 16, 1, 16, 2, 1280)


def solution(mesh):
    return jax.shard_map(
        per_device,
        mesh=mesh,
        in_specs=(
            P("section", None, "slab", None, None, None),
            P(),
            P(),
            P(),
            P(),
            P(),
            P(),
            P(),
            P(),
            P(),
            P(),
            P(),
            P("section", None),
            P("section", None),
            P("section", None, None, None, None),
            P("section", None),
        ),
        out_specs=P("section", None, "slab", None, None, None),
        check_vma=False,
    )
```
